32 devices in a mesh: row: 16 (over z, y, x), col: 2 (over core).
Axes of the slice: x: 2, y: 2, z: 4, core: 2. Of those that a mesh axis runs over, the one named last changes fastest.
Arguments:
- environment: float32 [6144, 6144], P('row', 'col'), may hold values from -6 to 6
- site_tensors: float32 [2, 6144, 6144], P(None, 'row', 'col'), may hold values from -0.078125 to 0.078125
- panel_offset: int32 [1], replicated, may hold values from 0 to 6016
Outputs:
- new_panel: float32 [128, 6144], P('row', 'col')
The draws below stay inside these ranges and needn't reach their ends.
All inputs are finite; a program needn't handle non-finite values.
Results may differ from the reference program's by a relative error of at most 0.0001.
Values sent between devices are 32-bit elements; how exact they have to be, the bound alone decides.
A program may use at most 64 MiB of HBM per device.

```python
import jax
import jax.numpy as jnp
from jax import lax

D = 6144
PHYS = 2
PANEL = 128


def block_levels(key, extent, cuts, least, high):
    def one(position, parts):
        heights = jax.random.uniform(jax.random.fold_in(jax.random.fold_in(key, 6), position), (parts,), jnp.float32, least / len(cuts), high / len(cuts))
        return jnp.repeat(jnp.exp(heights), extent[position] // parts).reshape((-1,) + (1,) * (len(extent) - position - 1))

    loudness = one(*cuts[0])
    for cut in cuts[1:]:
        loudness = loudness * one(*cut)
    return loudness


def bell_draw(own_key, shape, width, limit, shards=(), held_as=jnp.bfloat16):
    values = jax.random.normal(own_key, shape, jnp.float32) * width
    if len(shards) > 0:
        values = block_levels(own_key, shape, shards, -0.22, 0.18) * values
    return jnp.clip(values, min=-limit, max=limit).astype(held_as)


def setup_inputs(seed: int = 0) -> dict:
    seeds = jax.random.split(jax.random.key(seed), 4)
    return {
        "environment": bell_draw(seeds[0], (D, D), 1.0, 6.0, ((0, 16), (1, 2)), jnp.float32),
        "site_tensors": bell_draw(seeds[1], (PHYS, D, D), D ** -0.5, 0.078125, ((1, 16), (2, 2)), jnp.float32),
        "panel_offset": jax.random.randint(seeds[2], (1,), 0, D - PANEL + 1).astype(jnp.int32),
    }


def reference(environment, site_tensors, panel_offset):
    result = jnp.zeros((PANEL, D), jnp.float32)
    for phys in range(PHYS):
        columns = lax.dynamic_slice_in_dim(site_tensors[phys], panel_offset[0].astype(jnp.int32), PANEL, 1)
        bond_block = jnp.dot(columns.T, environment, precision=lax.Precision.HIGHEST, preferred_element_type=jnp.float32)
        result = result + jnp.dot(bond_block, site_tensors[phys], precision=lax.Precision.HIGHEST, preferred_element_type=jnp.float32)
    return result
```

```python
import functools

import jax
import jax.numpy as jnp
from jax import lax
from jax.experimental import pallas as pl
from jax.experimental.pallas import tpu as pltpu
from jax.sharding import PartitionSpec as P

PHYS = 2
PANEL = 128
STRIPES = 2
ORDER = (0, 3, 1, 2)
PAIRED = (2,)
STEPS = (
    ("Q", 0), ("SA", 0, 0), ("ZS", 2, 0, 0), ("SA", 1, 0), ("SA", 0, 1), ("Q", 1), ("SA", 1, 1), ("Q", 2), ("F", 0, 0),
    ("ZS", 2, 1, 2), ("F", 0, 1), ("ZS", 2, 0, 2), ("Q", 3), ("ZS", 2, 1, 0), ("F", 1, 0), ("ZS", 2, 1, 1), ("SA", 3, 0),
    ("ZS", 2, 1, 3), ("W", 1), ("C", 0, 0), ("W", 0), ("F", 1, 1), ("SA", 2, 0), ("SA", 3, 1), ("C", 0, 1), ("C", 1, 0),
    ("SA", 2, 1), ("F", 3, 0), ("ZS", 2, 0, 3), ("ZS", 2, 0, 1), ("ZB", 2, 1), ("F", 3, 1), ("R", 0, 0), ("R", 0, 1),
    ("ZC", 2, 1), ("C", 1, 1), ("ZC", 2, 0), ("F", 2, 1), ("D", 0), ("PD", 0, 0, 0), ("ZB", 2, 0), ("C", 3, 0), ("PD", 0, 0, 1),
    ("F", 2, 0), ("R", 1, 0), ("C", 3, 1), ("R", 1, 1), ("PD", 0, 1, 0), ("PD", 0, 1, 1), ("D", 1), ("PD", 1, 0, 0), ("C", 2, 1),
    ("PD", 1, 0, 1), ("R", 3, 0), ("C", 2, 0), ("PF", 0, 0, 1), ("PD", 1, 1, 0), ("PD", 1, 1, 1), ("PF", 0, 1, 1),
    ("PF", 1, 0, 0), ("R", 3, 1), ("PF", 1, 0, 1), ("PF", 0, 1, 0), ("PF", 0, 0, 0), ("R", 2, 1), ("D", 3), ("PD", 3, 0, 0),
    ("R", 2, 0), ("PF", 1, 1, 0), ("PD", 3, 0, 1), ("PF", 1, 1, 1), ("PD", 3, 1, 0), ("D", 2), ("PD", 2, 0, 0), ("PD", 2, 0, 1),
    ("PC", 0, 1, 1), ("PD", 2, 1, 0), ("PD", 3, 1, 1), ("PF", 3, 0, 0), ("PD", 2, 1, 1), ("PC", 1, 0, 1), ("PF", 3, 0, 1),
    ("PC", 0, 0, 1), ("PC", 1, 1, 0), ("PC", 0, 1, 0), ("PF", 2, 0, 1), ("PF", 2, 0, 0), ("PF", 2, 1, 0), ("PC", 1, 0, 0),
    ("PC", 1, 1, 1), ("PC", 3, 0, 0), ("PF", 3, 1, 1), ("PC", 0, 0, 0), ("PF", 2, 1, 1), ("PC", 3, 0, 1), ("PF", 3, 1, 0),
    ("PC", 2, 0, 1), ("PC", 2, 1, 0), ("PC", 3, 1, 1), ("PC", 2, 1, 1), ("PC", 2, 0, 0), ("PC", 3, 1, 0), ("PR", 0, 1, 1),
    ("PR", 3, 1, 1), ("PR", 2, 1, 0), ("PR", 1, 1, 0), ("PR", 2, 1, 1), ("PR", 0, 1, 0), ("PR", 2, 0, 1), ("PR", 0, 0, 0),
    ("PR", 0, 0, 1), ("PR", 3, 0, 0), ("PR", 3, 1, 0), ("PR", 1, 1, 1), ("PR", 3, 0, 1), ("PR", 1, 0, 0), ("PR", 1, 0, 1),
    ("PR", 2, 0, 0),
)
F32 = jnp.float32
BF16 = jnp.bfloat16


def split(value):
    high = value.astype(BF16)
    return high, (value - high.astype(F32)).astype(BF16)


def dot3(lhs, rhs_high, rhs_low):
    count = lhs.shape[0] // 2
    dot = functools.partial(jnp.dot, preferred_element_type=F32)
    both = dot(lhs, rhs_high)
    return both[:count] + (both[count:] + dot(lhs[:count], rhs_low))


class Place:
    def __init__(self):
        row = lax.axis_index("row")
        self.col = lax.axis_index("col")
        self.x, self.y, self.z = row % 2, (row // 2) % 2, row // 4
        self.owner = self.z // 2 == self.col

    def at(self, x=None, y=None, z=None, col=None):
        x, y, z = (self.x if x is None else x), (self.y if y is None else y), (self.z if z is None else z)
        return (z * 4 + y * 2 + x, self.col if col is None else col)

    def quarter(self, i):
        return [(1 - self.y, 1 - self.x), (1 - self.y, self.x), (self.y, 1 - self.x), (self.y, self.x)][i]

    def first_link(self, half):
        return self.at(x=1 - self.x) if half == 0 else self.at(y=1 - self.y)

    def second_link(self, half):
        return self.at(y=1 - self.y) if half == 0 else self.at(x=1 - self.x)

    def passed(self, half):
        return self.quarter(1 if half == 0 else 2)

    def last(self, half):
        return self.quarter(2 if half == 0 else 1)


def send(src, dst, send_sem, recv_sem, device):
    return pltpu.make_async_remote_copy(
        src_ref=src, dst_ref=dst, send_sem=send_sem, recv_sem=recv_sem, device_id=device, device_id_type=pl.DeviceIdType.MESH
    )


class Bond:
    def __init__(self, place, refs):
        self.place = place
        (self.parts, self.first, self.total, self.second, self.done, self.third, self.pair, self.block) = refs[:8]
        (self.xy_send, self.xy_recv, self.z_send, self.z_recv, self.pair_send, self.pair_recv, self.send, self.recv) = refs[8:]
        self.kept = place.z % 2

    @staticmethod
    def scratch(depth, height, width):
        return [
            pltpu.VMEM((PHYS, depth, 2, 2, 2, height, width), F32),
            pltpu.VMEM((PHYS, depth, 2, 2, height, width), F32),
            pltpu.VMEM((PHYS, depth, 2, height, width), F32),
            pltpu.VMEM((PHYS, depth, 2, height, width), F32),
            pltpu.VMEM((PHYS, depth, 2, height, width), F32),
            pltpu.VMEM((PHYS, depth, depth, height, width), F32),
            pltpu.VMEM((PHYS, max(len(PAIRED), 1), 4, height, width), F32),
            pltpu.VMEM((PHYS, depth, height, width), F32),
        ] + [
            pltpu.SemaphoreType.DMA(shape)
            for shape in [(PHYS, depth, 3)] * 2
            + [(PHYS, depth, 2), (PHYS, depth, depth)]
            + [(PHYS, max(len(PAIRED), 1), 4)] * 2
            + [(PHYS, depth)] * 2
        ]

    def slots(self, k):
        return 1 if k in PAIRED else 2

    def part(self, h, k, at):
        y, x = at
        return (h, k, self.kept, y, x) if k in PAIRED else (h, k, slice(None), y, x)

    def landing(self, ref, h, k, *rest):
        return ref.at[(h, k, *rest, 0)] if k in PAIRED else ref.at[(h, k, *rest)]

    def hop(self, h, k, n):
        here, sems = self.place, (self.xy_send.at[h, k, n], self.xy_recv.at[h, k, n])
        if n == 2:
            return send(self.landing(self.total, h, k), self.landing(self.second, h, k), *sems, here.second_link(h))
        src = self.parts.at[self.part(h, k, here.quarter(0) if n == 0 else here.last(h))]
        return send(src, self.landing(self.first, h, k, n), *sems, here.first_link(h))

    def halve(self, h, k, i):
        here, n = self.place, PAIRED.index(k)
        y, x = here.quarter(i)
        partner = here.at(z=here.z + 1 - 2 * self.kept)
        return send(
            self.parts.at[h, k, 1 - self.kept, y, x],
            self.pair.at[h, n, i],
            self.pair_send.at[h, n, i],
            self.pair_recv.at[h, n, i],
            partner,
        )

    def add_pair(self, h, k, i):
        self.halve(h, k, i).wait_recv()
        at = self.part(h, k, self.place.quarter(i))
        self.parts[at] = self.parts[at] + self.pair[h, PAIRED.index(k), i]

    def across(self, h, k, slot, z):
        here = self.place
        return send(
            self.done.at[h, k, slot],
            self.third.at[h, k, here.z],
            self.z_send.at[h, k, slot],
            self.z_recv.at[h, k, here.z],
            here.at(z=z),
        )

    def arrival(self, h, k, source):
        return send(
            self.done.at[h, k, 0], self.third.at[h, k, source], self.z_send.at[h, k, 0], self.z_recv.at[h, k, source], self.place.at(z=source)
        )

    def share(self, h, k):
        here = self.place
        return send(self.block.at[h, k], self.block.at[h, k], self.send.at[h, k], self.recv.at[h, k], here.at(col=1 - here.col))

    def start(self, h, k):
        if k in PAIRED:
            self.add_pair(h, k, 0)
        self.hop(h, k, 0).start()

    def forward(self, h, k):
        y, x = self.place.passed(h)
        self.hop(h, k, 0).wait_recv()
        for slot in range(self.slots(k)):
            mine = self.kept if k in PAIRED else slot
            self.total[h, k, slot] = self.parts[h, k, mine, y, x] + self.first[h, k, 0, slot]
        self.hop(h, k, 2).start()
        self.hop(h, k, 1).start()

    def leave(self, h, k):
        here = self.place
        if k in PAIRED:
            return [], [(0, here.z + 2 - 4 * (here.z // 2))]
        other = 1 - self.kept
        return [(other, here.col * 2 + other)], [(self.kept, here.col * 2 + self.kept)]

    def finish_xy(self, h, k):
        here = self.place
        y, x = here.quarter(3)
        if k in PAIRED:
            self.add_pair(h, k, 3)
        self.hop(h, k, 1).wait_recv()
        self.hop(h, k, 2).wait_recv()
        for slot in range(self.slots(k)):
            mine = self.kept if k in PAIRED else slot
            self.done[h, k, slot] = (self.parts[h, k, mine, y, x] + self.first[h, k, 1, slot]) + self.second[h, k, slot]
        always, unowned = self.leave(h, k)
        for slot, z in always:
            self.across(h, k, slot, z).start()

        @pl.when(jnp.logical_not(here.owner))
        def _():
            for slot, z in unowned:
                self.across(h, k, slot, z).start()

    def result(self, h, k):
        here = self.place

        @pl.when(here.owner)
        def _():
            value = self.done[h, k, 0 if k in PAIRED else self.kept]
            for j in (2,) if k in PAIRED else (1, 3, 2):
                source = (here.z + j) % 4
                self.arrival(h, k, source).wait_recv()
                value = value + self.third[h, k, source]
            self.block[h, k] = value
            self.share(h, k).start()

    def fetch(self, k):
        @pl.when(jnp.logical_not(self.place.owner))
        def _():
            for h in range(PHYS):
                self.share(h, k).wait_recv()

    def drain(self):
        here = self.place
        for k in range(4):

            def one(h, carry):
                for n in range(3):
                    self.hop_sent(h, k, n)
                always, unowned = self.leave(h, k)
                for slot, z in always:
                    self.across(h, k, slot, z).wait_send()

                @pl.when(jnp.logical_not(here.owner))
                def _():
                    for slot, z in unowned:
                        self.across(h, k, slot, z).wait_send()

                @pl.when(here.owner)
                def _():
                    self.share(h, k).wait_send()

                if k in PAIRED:
                    for i in range(4):
                        self.halve(h, k, i).wait_send()
                return carry

            lax.fori_loop(0, PHYS, one, 0)

    def hop_sent(self, h, k, n):
        here = self.place
        src = self.landing(self.total, h, k)
        dst = self.landing(self.second, h, k)
        send(src, dst, self.xy_send.at[h, k, n], self.xy_recv.at[h, k, n], here.at(x=1 - here.x)).wait_send()


class Panel:
    def __init__(self, place, refs):
        self.place = place
        self.parts, self.first, self.total, self.second, self.done, self.third = refs[:6]
        self.xy_send, self.xy_recv, self.z_send, self.z_recv = refs[6:]
        self.width = self.parts.shape[-1]

    @staticmethod
    def scratch(depth, height, width):
        one = pltpu.VMEM((depth, 2, STRIPES, height, width), F32)
        return [
            pltpu.VMEM((depth, 2, STRIPES, 2, 2, height, width), F32),
            pltpu.VMEM((depth, 2, STRIPES, 2, height, width), F32),
            one,
            one,
            one,
            pltpu.VMEM((2, STRIPES, depth, height, width), F32),
        ] + [
            pltpu.SemaphoreType.DMA(shape)
            for shape in [(depth, 2, STRIPES, 3)] * 2 + [(depth, 2, STRIPES), (2, STRIPES, depth)]
        ]

    def columns(self, st, h):
        return pl.ds((h * STRIPES + st) * self.width, self.width)

    def hop(self, g, st, h, n):
        here, sems = self.place, (self.xy_send.at[g, h, st, n], self.xy_recv.at[g, h, st, n])
        if n == 2:
            return send(self.total.at[g, h, st], self.second.at[g, h, st], *sems, here.second_link(h))
        y, x = here.quarter(0) if n == 0 else here.last(h)
        return send(self.parts.at[g, h, st, y, x], self.first.at[g, h, st, n], *sems, here.first_link(h))

    def across(self, g, st, h, source):
        return send(
            self.done.at[g, h, st],
            self.third.at[h, st, source],
            self.z_send.at[g, h, st],
            self.z_recv.at[h, st, source],
            self.place.at(z=ORDER[g]),
        )

    def arrival(self, g, st, h, source):
        return send(
            self.done.at[g, h, st],
            self.third.at[h, st, source],
            self.z_send.at[g, h, st],
            self.z_recv.at[h, st, source],
            self.place.at(z=source),
        )

    def start(self, g, st, h, product):
        self.parts[g, h, st] = product.reshape(self.parts.shape[3:])
        self.hop(g, st, h, 0).start()

    def forward(self, g, st, h):
        y, x = self.place.passed(h)
        self.hop(g, st, h, 0).wait_recv()
        self.total[g, h, st] = self.parts[g, h, st, y, x] + self.first[g, h, st, 0]
        self.hop(g, st, h, 2).start()
        self.hop(g, st, h, 1).start()

    def finish_xy(self, g, st, h):
        here = self.place
        y, x = here.quarter(3)
        self.hop(g, st, h, 1).wait_recv()
        self.hop(g, st, h, 2).wait_recv()
        self.done[g, h, st] = (self.parts[g, h, st, y, x] + self.first[g, h, st, 1]) + self.second[g, h, st]

        @pl.when(here.z != ORDER[g])
        def _():
            self.across(g, st, h, here.z).start()

    def result(self, g, st, h, out):
        here = self.place

        @pl.when(here.z == ORDER[g])
        def _():
            value = self.done[g, h, st]
            for j in (1, 3, 2):
                source = (here.z + j) % 4
                self.arrival(g, st, h, source).wait_recv()
                value = value + self.third[h, st, source]
            out[:, self.columns(st, h)] = value

    def drain(self):
        here = self.place

        def sent(g, carry):
            for st in range(STRIPES):
                for h in range(2):
                    for n in range(3):
                        send(
                            self.total.at[g, h, st],
                            self.second.at[g, h, st],
                            self.xy_send.at[g, h, st, n],
                            self.xy_recv.at[g, h, st, n],
                            here.at(x=1 - here.x),
                        ).wait_send()
            return carry

        lax.fori_loop(0, len(ORDER), sent, 0)
        for g in range(len(ORDER)):

            @pl.when(here.z != ORDER[g])
            def _():
                for st in range(STRIPES):
                    for h in range(2):
                        self.across(g, st, h, here.z).wait_send()


def kernel(window, env_hbm, site_hbm, out, env, site, high_site, low_site, windows, pan, lhs, *rest):
    env_sem, site_sem, win_send, win_recv = rest[:4]
    bond_refs, panel_refs = rest[4:20], rest[20:30]
    here = Place()
    barrier = pltpu.get_barrier_semaphore()
    partners = [here.at(col=1 - here.col), here.at(x=1 - here.x), here.at(y=1 - here.y)]
    partners += [here.at(z=(here.z + j) % 4) for j in range(1, 4)]
    for partner in partners:
        pl.semaphore_signal(barrier, inc=1, device_id=partner, device_id_type=pl.DeviceIdType.MESH)

    depth_local = env.shape[0]
    bond, panel = Bond(here, bond_refs), Panel(here, panel_refs)
    height = bond.block.shape[2]

    def env_columns(i, slot):
        y, x = here.quarter(i)
        return pl.ds(pl.multiple_of((slot * 4 + y * 2 + x) * depth_local, 128), depth_local)

    def env_load(i, slot):
        at = (slice(None), env_columns(i, slot))
        return pltpu.make_async_copy(env_hbm.at[at], env.at[at], env_sem.at[i, slot])

    def site_load(phys):
        return pltpu.make_async_copy(site_hbm.at[phys], site.at[phys], site_sem.at[phys])

    for i in range(4):
        for slot in range(2):
            env_load(i, slot).start()
    for phys in range(PHYS):
        site_load(phys).start()

    exchange = send(window, windows, win_send, win_recv, here.at(col=1 - here.col))
    pl.semaphore_wait(barrier, len(partners))
    exchange.start()
    exchange.wait_recv()
    for phys in range(PHYS):
        flipped = (window[phys] + windows[phys]).T
        for k, z in enumerate(ORDER):
            at = phys * PANEL + k * height
            high, low = split(flipped[z * height : (z + 1) * height])
            pan[at : at + height, :] = high
            pan[PHYS * PANEL + at : PHYS * PANEL + at + height, :] = low

    def quarter_block(i):
        y, x = here.quarter(i)
        for slot in range(2):
            env_load(i, slot).wait()

        def one(slot, carry):
            product = dot3(pan[...], *split(env[:, env_columns(i, slot)]))
            product = product.reshape(PHYS, len(ORDER), height, depth_local)
            for phys in range(PHYS):
                for k in range(len(ORDER)):
                    bond.parts[phys, k, slot, y, x] = product[phys, k]
            return carry

        lax.fori_loop(0, 2, one, 0)

    step = 16

    def split_site(phys):
        site_load(phys).wait()

        def one(i, carry):
            at = pl.ds(pl.multiple_of(i * step, step), step)
            to = pl.ds(pl.multiple_of(phys * depth_local + i * step, step), step)
            high_site[to, :], low_site[to, :] = split(site[phys, at, :])
            return carry

        lax.fori_loop(0, depth_local // step, one, 0)

    def gather_block(g):
        bond.fetch(g)
        lhs[g] = jnp.concatenate(split(jnp.concatenate([bond.block[phys, g] for phys in range(PHYS)], axis=1)), axis=0)

    def panel_product(g, st, h):
        columns = panel.columns(st, h)
        panel.start(g, st, h, dot3(lhs[g], high_site[:, columns], low_site[:, columns]))

    run = {
        "Q": quarter_block,
        "W": split_site,
        "ZS": lambda k, h, i: bond.halve(h, k, i).start(),
        "ZB": lambda k, h: bond.add_pair(h, k, 1),
        "ZC": lambda k, h: bond.add_pair(h, k, 2),
        "SA": lambda k, h: bond.start(h, k),
        "F": lambda k, h: bond.forward(h, k),
        "C": lambda k, h: bond.finish_xy(h, k),
        "R": lambda k, h: bond.result(h, k),
        "D": gather_block,
        "PD": panel_product,
        "PF": panel.forward,
        "PC": panel.finish_xy,
        "PR": lambda g, st, h: panel.result(g, st, h, out),
    }
    for name, *at in STEPS:
        run[name](*at)

    exchange.wait_send()
    bond.drain()
    panel.drain()


def panel_window(site_tensors, panel_offset):
    cols_local = site_tensors.shape[2]
    padded = jnp.pad(site_tensors, ((0, 0), (0, 0), (PANEL, PANEL)))
    slice_start = jnp.clip(panel_offset[0] - lax.axis_index("col") * cols_local + PANEL, 0, cols_local + PANEL)
    return lax.dynamic_slice_in_dim(padded, slice_start, PANEL, 2)


def one_kernel(environment, site_tensors, panel_offset):
    depth_local, cols_local = environment.shape
    depth = len(ORDER)
    height = PANEL // depth
    any_space = pl.BlockSpec(memory_space=pl.ANY)
    in_vmem = pl.BlockSpec(memory_space=pltpu.VMEM)
    return pl.pallas_call(
        kernel,
        out_shape=jax.ShapeDtypeStruct((height // 4, cols_local), F32),
        in_specs=[in_vmem, any_space, any_space],
        out_specs=in_vmem,
        scratch_shapes=[
            pltpu.VMEM(environment.shape, F32),
            pltpu.VMEM(site_tensors.shape, F32),
            pltpu.VMEM((PHYS * depth_local, cols_local), BF16),
            pltpu.VMEM((PHYS * depth_local, cols_local), BF16),
            pltpu.VMEM((PHYS, depth_local, PANEL), F32),
            pltpu.VMEM((2 * PHYS * PANEL, depth_local), BF16),
            pltpu.VMEM((depth, 2 * height, PHYS * depth_local), BF16),
            pltpu.SemaphoreType.DMA((4, 2)),
            pltpu.SemaphoreType.DMA((PHYS,)),
            pltpu.SemaphoreType.DMA,
            pltpu.SemaphoreType.DMA,
        ]
        + Bond.scratch(depth, height, depth_local)
        + Panel.scratch(depth, height // 4, cols_local // (2 * STRIPES)),
        compiler_params=pltpu.CompilerParams(collective_id=0, has_side_effects=True, vmem_limit_bytes=60 * 1024 * 1024),
    )(panel_window(site_tensors, panel_offset), environment, site_tensors)


def collectives(environment, site_tensors, panel_offset):
    rows_local, cols_local = environment.shape
    col_index = lax.axis_index("col")
    panel_rows = lax.psum(panel_window(site_tensors, panel_offset), "col")
    first_col = lax.axis_index("row") * rows_local
    owner_col = first_col // cols_local
    owner_mask = (col_index == owner_col).astype(F32)
    accumulated = jnp.zeros((PANEL, cols_local), F32)
    for phys in range(PHYS):
        partial_one = jnp.dot(
            panel_rows[phys].T, environment, precision=lax.Precision.HIGHEST, preferred_element_type=F32
        )
        block_one = lax.dynamic_slice_in_dim(lax.psum(partial_one, "row"), first_col - owner_col * cols_local, rows_local, 1)
        fetched_one = lax.psum(block_one * owner_mask, "col")
        accumulated = accumulated + jnp.dot(
            fetched_one, site_tensors[phys], precision=lax.Precision.HIGHEST, preferred_element_type=F32
        )
    return lax.psum_scatter(accumulated, "row", scatter_dimension=0, tiled=True)


def solution(mesh):
    rows, cols = mesh.shape["row"], mesh.shape["col"]

    def shards(environment, site_tensors, panel_offset):
        depth_local, cols_local = environment.shape
        fits = (
            rows == 4 * len(ORDER)
            and cols == 2
            and depth_local % 128 == 0
            and cols_local == 8 * depth_local
            and cols_local % (2 * STRIPES * 128) == 0
            and PANEL % (8 * rows) == 0
        )
        if fits:
            return one_kernel(environment, site_tensors, panel_offset)
        return collectives(environment, site_tensors, panel_offset)

    return jax.shard_map(
        shards,
        mesh=mesh,
        in_specs=(P("row", "col"), P(None, "row", "col"), P()),
        out_specs=P("row", "col"),
        check_vma=False,
    )
```

```python
import functools

import jax
import jax.numpy as jnp
from jax import lax
from jax.experimental import pallas as pl
from jax.experimental.pallas import tpu as pltpu
from jax.sharding import PartitionSpec as P

PHYS = 2
PANEL = 128
STRIPES = 3
ORDER = (0, 3, 1, 2)
PAIRED = ((1, 0), (2, 0), (2, 1))
STEPS = (
    ("Q", 0), ("SA", 0, 1), ("SA", 0, 0), ("ZS", 1, 0, 0), ("SA", 3, 0), ("Q", 1), ("ZS", 1, 0, 1), ("SA", 1, 1), ("Q", 2),
    ("ZS", 1, 0, 2), ("W", 1), ("ZS", 2, 1, 2), ("Q", 3), ("SA", 1, 0), ("ZS", 2, 0, 1), ("SA", 3, 1), ("ZS", 2, 0, 0),
    ("ZS", 2, 0, 2), ("ZS", 2, 1, 0), ("ZS", 2, 1, 1), ("F", 0, 0), ("ZB", 1, 0), ("ZS", 2, 1, 3), ("ZC", 1, 0), ("F", 0, 1),
    ("ZS", 1, 0, 3), ("F", 3, 1), ("ZB", 2, 0), ("SA", 2, 0), ("F", 3, 0), ("ZC", 2, 0), ("C", 0, 0), ("C", 0, 1), ("F", 1, 0),
    ("F", 1, 1), ("ZB", 2, 1), ("C", 3, 1), ("W", 0), ("SA", 2, 1), ("R", 0, 0), ("C", 3, 0), ("ZS", 2, 0, 3), ("R", 0, 1),
    ("F", 2, 0), ("ZC", 2, 1), ("D", 0), ("PD", 0, 0, 0), ("C", 1, 0), ("PD", 0, 0, 1), ("C", 1, 1), ("R", 3, 1), ("F", 2, 1),
    ("PD", 0, 1, 0), ("PD", 0, 1, 1), ("R", 3, 0), ("PF", 0, 0, 1), ("C", 2, 0), ("PD", 0, 2, 0), ("D", 3), ("PD", 3, 0, 0),
    ("PD", 3, 0, 1), ("PD", 0, 2, 1), ("PD", 3, 1, 0), ("PF", 0, 0, 0), ("R", 1, 0), ("C", 2, 1), ("R", 1, 1), ("PD", 3, 1, 1),
    ("PF", 0, 1, 1), ("PD", 3, 2, 0), ("PD", 3, 2, 1), ("PF", 0, 1, 0), ("D", 1), ("PD", 1, 0, 0), ("PD", 1, 0, 1),
    ("PF", 3, 0, 1), ("PD", 1, 1, 0), ("PD", 1, 1, 1), ("PF", 3, 1, 0), ("R", 2, 0), ("PF", 3, 0, 0), ("PD", 1, 2, 0),
    ("PF", 0, 2, 1), ("PF", 0, 2, 0), ("R", 2, 1), ("PD", 1, 2, 1), ("PF", 3, 1, 1), ("PC", 0, 0, 1), ("PF", 1, 0, 0), ("D", 2),
    ("PD", 2, 0, 0), ("PD", 2, 0, 1), ("PF", 1, 1, 0), ("PD", 2, 1, 0), ("PD", 2, 1, 1), ("PC", 3, 0, 1), ("PC", 3, 1, 0),
    ("PF", 1, 1, 1), ("PC", 3, 0, 0), ("PF", 1, 2, 0), ("PD", 2, 2, 0), ("PD", 2, 2, 1), ("PF", 3, 2, 0), ("PC", 0, 0, 0),
    ("PF", 1, 2, 1), ("PC", 0, 1, 1), ("PC", 0, 1, 0), ("PC", 0, 2, 1), ("PC", 1, 0, 0), ("PF", 2, 0, 0), ("PF", 2, 0, 1),
    ("PC", 3, 1, 1), ("PF", 2, 1, 0), ("PC", 1, 1, 0), ("PC", 0, 2, 0), ("PF", 2, 1, 1), ("PF", 1, 0, 1), ("PF", 2, 2, 0),
    ("PC", 1, 2, 0), ("PF", 3, 2, 1), ("PF", 2, 2, 1), ("PC", 1, 1, 1), ("PC", 3, 2, 0), ("PC", 2, 0, 0), ("PC", 2, 0, 1),
    ("PC", 2, 1, 0), ("PC", 1, 2, 1), ("PC", 2, 1, 1), ("PC", 2, 2, 0), ("PC", 1, 0, 1), ("PC", 2, 2, 1), ("PC", 3, 2, 1),
    ("PR", 3, 0, 1), ("PR", 3, 0, 0), ("PR", 3, 1, 0), ("PR", 0, 0, 0), ("PR", 2, 0, 0), ("PR", 2, 1, 1), ("PR", 2, 1, 0),
    ("PR", 1, 2, 0), ("PR", 3, 2, 0), ("PR", 1, 0, 1), ("PR", 2, 0, 1), ("PR", 0, 2, 1), ("PR", 3, 2, 1), ("PR", 1, 1, 1),
    ("PR", 1, 2, 1), ("PR", 3, 1, 1), ("PR", 2, 2, 0), ("PR", 0, 2, 0), ("PR", 0, 1, 0), ("PR", 1, 0, 0), ("PR", 2, 2, 1),
    ("PR", 0, 1, 1), ("PR", 1, 1, 0), ("PR", 0, 0, 1),
)
F32 = jnp.float32
BF16 = jnp.bfloat16


def split(value):
    high = value.astype(BF16)
    return high, (value - high.astype(F32)).astype(BF16)


def dot3(lhs, rhs_high, rhs_low):
    count = lhs.shape[0] // 2
    dot = functools.partial(jnp.dot, preferred_element_type=F32)
    both = dot(lhs, rhs_high)
    return both[:count] + (both[count:] + dot(lhs[:count], rhs_low))


class Place:
    def __init__(self):
        row = lax.axis_index("row")
        self.col = lax.axis_index("col")
        self.x, self.y, self.z = row % 2, (row // 2) % 2, row // 4
        self.owner = self.z // 2 == self.col

    def at(self, x=None, y=None, z=None, col=None):
        x, y, z = (self.x if x is None else x), (self.y if y is None else y), (self.z if z is None else z)
        return (z * 4 + y * 2 + x, self.col if col is None else col)

    def quarter(self, i):
        return [(1 - self.y, 1 - self.x), (1 - self.y, self.x), (self.y, 1 - self.x), (self.y, self.x)][i]

    def first_link(self, half):
        return self.at(x=1 - self.x) if half == 0 else self.at(y=1 - self.y)

    def second_link(self, half):
        return self.at(y=1 - self.y) if half == 0 else self.at(x=1 - self.x)

    def passed(self, half):
        return self.quarter(1 if half == 0 else 2)

    def last(self, half):
        return self.quarter(2 if half == 0 else 1)


def send(src, dst, send_sem, recv_sem, device):
    return pltpu.make_async_remote_copy(
        src_ref=src, dst_ref=dst, send_sem=send_sem, recv_sem=recv_sem, device_id=device, device_id_type=pl.DeviceIdType.MESH
    )


class Bond:
    def __init__(self, place, refs):
        self.place = place
        (self.parts, self.first, self.total, self.second, self.done, self.third, self.pair, self.block) = refs[:8]
        (self.xy_send, self.xy_recv, self.z_send, self.z_recv, self.pair_send, self.pair_recv, self.send, self.recv) = refs[8:]
        self.kept = place.z % 2

    @staticmethod
    def scratch(depth, height, width):
        return [
            pltpu.VMEM((PHYS, depth, 2, 2, 2, height, width), F32),
            pltpu.VMEM((PHYS, depth, 2, 2, height, width), F32),
            pltpu.VMEM((PHYS, depth, 2, height, width), F32),
            pltpu.VMEM((PHYS, depth, 2, height, width), F32),
            pltpu.VMEM((PHYS, depth, 2, height, width), F32),
            pltpu.VMEM((PHYS, depth, depth, height, width), F32),
            pltpu.VMEM((max(len(PAIRED), 1), 4, height, width), F32),
            pltpu.VMEM((PHYS, depth, height, width), F32),
        ] + [
            pltpu.SemaphoreType.DMA(shape)
            for shape in [(PHYS, depth, 3)] * 2
            + [(PHYS, depth, 2), (PHYS, depth, depth)]
            + [(max(len(PAIRED), 1), 4)] * 2
            + [(PHYS, depth)] * 2
        ]

    def slots(self, h, k):
        return 1 if (k, h) in PAIRED else 2

    def part(self, h, k, at):
        y, x = at
        return (h, k, self.kept, y, x) if (k, h) in PAIRED else (h, k, slice(None), y, x)

    def landing(self, ref, h, k, *rest):
        return ref.at[(h, k, *rest, 0)] if (k, h) in PAIRED else ref.at[(h, k, *rest)]

    def hop(self, h, k, n):
        here, sems = self.place, (self.xy_send.at[h, k, n], self.xy_recv.at[h, k, n])
        if n == 2:
            return send(self.landing(self.total, h, k), self.landing(self.second, h, k), *sems, here.second_link(h))
        src = self.parts.at[self.part(h, k, here.quarter(0) if n == 0 else here.last(h))]
        return send(src, self.landing(self.first, h, k, n), *sems, here.first_link(h))

    def halve(self, h, k, i):
        here, n = self.place, PAIRED.index((k, h))
        y, x = here.quarter(i)
        partner = here.at(z=here.z + 1 - 2 * self.kept)
        return send(
            self.parts.at[h, k, 1 - self.kept, y, x],
            self.pair.at[n, i],
            self.pair_send.at[n, i],
            self.pair_recv.at[n, i],
            partner,
        )

    def add_pair(self, h, k, i):
        self.halve(h, k, i).wait_recv()
        at = self.part(h, k, self.place.quarter(i))
        self.parts[at] = self.parts[at] + self.pair[PAIRED.index((k, h)), i]

    def across(self, h, k, slot, z):
        here = self.place
        return send(
            self.done.at[h, k, slot],
            self.third.at[h, k, here.z],
            self.z_send.at[h, k, slot],
            self.z_recv.at[h, k, here.z],
            here.at(z=z),
        )

    def arrival(self, h, k, source):
        return send(
            self.done.at[h, k, 0], self.third.at[h, k, source], self.z_send.at[h, k, 0], self.z_recv.at[h, k, source], self.place.at(z=source)
        )

    def share(self, h, k):
        here = self.place
        return send(self.block.at[h, k], self.block.at[h, k], self.send.at[h, k], self.recv.at[h, k], here.at(col=1 - here.col))

    def start(self, h, k):
        if (k, h) in PAIRED:
            self.add_pair(h, k, 0)
        self.hop(h, k, 0).start()

    def forward(self, h, k):
        y, x = self.place.passed(h)
        self.hop(h, k, 0).wait_recv()
        for slot in range(self.slots(h, k)):
            mine = self.kept if (k, h) in PAIRED else slot
            self.total[h, k, slot] = self.parts[h, k, mine, y, x] + self.first[h, k, 0, slot]
        self.hop(h, k, 2).start()
        self.hop(h, k, 1).start()

    def leave(self, h, k):
        here = self.place
        if (k, h) in PAIRED:
            return [], [(0, here.z + 2 - 4 * (here.z // 2))]
        other = 1 - self.kept
        return [(other, here.col * 2 + other)], [(self.kept, here.col * 2 + self.kept)]

    def finish_xy(self, h, k):
        here = self.place
        y, x = here.quarter(3)
        if (k, h) in PAIRED:
            self.add_pair(h, k, 3)
        self.hop(h, k, 1).wait_recv()
        self.hop(h, k, 2).wait_recv()
        for slot in range(self.slots(h, k)):
            mine = self.kept if (k, h) in PAIRED else slot
            self.done[h, k, slot] = (self.parts[h, k, mine, y, x] + self.first[h, k, 1, slot]) + self.second[h, k, slot]
        always, unowned = self.leave(h, k)
        for slot, z in always:
            self.across(h, k, slot, z).start()

        @pl.when(jnp.logical_not(here.owner))
        def _():
            for slot, z in unowned:
                self.across(h, k, slot, z).start()

    def result(self, h, k):
        here = self.place

        @pl.when(here.owner)
        def _():
            value = self.done[h, k, 0 if (k, h) in PAIRED else self.kept]
            for j in (2,) if (k, h) in PAIRED else (1, 3, 2):
                source = (here.z + j) % 4
                self.arrival(h, k, source).wait_recv()
                value = value + self.third[h, k, source]
            self.block[h, k] = value
            self.share(h, k).start()

    def fetch(self, k):
        @pl.when(jnp.logical_not(self.place.owner))
        def _():
            for h in range(PHYS):
                self.share(h, k).wait_recv()

    def drain(self):
        here = self.place
        for k, h in [(k, h) for k in range(len(ORDER)) for h in range(PHYS)]:
            for n in range(3):
                self.hop(h, k, n).wait_send()
            always, unowned = self.leave(h, k)
            for slot, z in always:
                self.across(h, k, slot, z).wait_send()

            @pl.when(jnp.logical_not(here.owner))
            def _():
                for slot, z in unowned:
                    self.across(h, k, slot, z).wait_send()

            @pl.when(here.owner)
            def _():
                self.share(h, k).wait_send()

            if (k, h) in PAIRED:
                for i in range(4):
                    self.halve(h, k, i).wait_send()


class Panel:
    def __init__(self, place, refs):
        self.place = place
        self.parts, self.first, self.total, self.second, self.done, self.third = refs[:6]
        self.xy_send, self.xy_recv, self.z_send, self.z_recv = refs[6:]
        self.width = self.parts.shape[-1]

    @staticmethod
    def scratch(depth, height, width):
        one = pltpu.VMEM((depth, 2, STRIPES, height, width), F32)
        return [
            pltpu.VMEM((depth, 2, STRIPES, 2, 2, height, width), F32),
            pltpu.VMEM((depth, 2, STRIPES, 2, height, width), F32),
            one,
            one,
            one,
            pltpu.VMEM((2, STRIPES, depth, height, width), F32),
        ] + [
            pltpu.SemaphoreType.DMA(shape)
            for shape in [(depth, 2, STRIPES, 3)] * 2 + [(depth, 2, STRIPES), (2, STRIPES, depth)]
        ]

    def columns(self, st, h):
        return pl.ds((h * STRIPES + st) * self.width, self.width)

    def hop(self, g, st, h, n):
        here, sems = self.place, (self.xy_send.at[g, h, st, n], self.xy_recv.at[g, h, st, n])
        if n == 2:
            return send(self.total.at[g, h, st], self.second.at[g, h, st], *sems, here.second_link(h))
        y, x = here.quarter(0) if n == 0 else here.last(h)
        return send(self.parts.at[g, h, st, y, x], self.first.at[g, h, st, n], *sems, here.first_link(h))

    def across(self, g, st, h, source):
        return send(
            self.done.at[g, h, st],
            self.third.at[h, st, source],
            self.z_send.at[g, h, st],
            self.z_recv.at[h, st, source],
            self.place.at(z=ORDER[g]),
        )

    def arrival(self, g, st, h, source):
        return send(
            self.done.at[g, h, st],
            self.third.at[h, st, source],
            self.z_send.at[g, h, st],
            self.z_recv.at[h, st, source],
            self.place.at(z=source),
        )

    def start(self, g, st, h, product):
        self.parts[g, h, st] = product.reshape(self.parts.shape[3:])
        self.hop(g, st, h, 0).start()

    def forward(self, g, st, h):
        y, x = self.place.passed(h)
        self.hop(g, st, h, 0).wait_recv()
        self.total[g, h, st] = self.parts[g, h, st, y, x] + self.first[g, h, st, 0]
        self.hop(g, st, h, 2).start()
        self.hop(g, st, h, 1).start()

    def finish_xy(self, g, st, h):
        here = self.place
        y, x = here.quarter(3)
        self.hop(g, st, h, 1).wait_recv()
        self.hop(g, st, h, 2).wait_recv()
        self.done[g, h, st] = (self.parts[g, h, st, y, x] + self.first[g, h, st, 1]) + self.second[g, h, st]

        @pl.when(here.z != ORDER[g])
        def _():
            self.across(g, st, h, here.z).start()

    def result(self, g, st, h, out):
        here = self.place

        @pl.when(here.z == ORDER[g])
        def _():
            value = self.done[g, h, st]
            for j in (1, 3, 2):
                source = (here.z + j) % 4
                self.arrival(g, st, h, source).wait_recv()
                value = value + self.third[h, st, source]
            out[:, self.columns(st, h)] = value

    def drain(self):
        here = self.place

        def sent(g, carry):
            for st in range(STRIPES):
                for h in range(2):
                    for n in range(3):
                        send(
                            self.total.at[g, h, st],
                            self.second.at[g, h, st],
                            self.xy_send.at[g, h, st, n],
                            self.xy_recv.at[g, h, st, n],
                            here.at(x=1 - here.x),
                        ).wait_send()
            return carry

        lax.fori_loop(0, len(ORDER), sent, 0)
        for g in range(len(ORDER)):

            @pl.when(here.z != ORDER[g])
            def _():
                for st in range(STRIPES):
                    for h in range(2):
                        self.across(g, st, h, here.z).wait_send()


def kernel(window, env_hbm, site_hbm, out, env, site, high_site, low_site, windows, pan, lhs, *rest):
    env_sem, site_sem, win_send, win_recv = rest[:4]
    bond_refs, panel_refs = rest[4:20], rest[20:30]
    here = Place()
    barrier = pltpu.get_barrier_semaphore()
    partners = [here.at(col=1 - here.col), here.at(x=1 - here.x), here.at(y=1 - here.y)]
    partners += [here.at(z=(here.z + j) % 4) for j in range(1, 4)]
    for partner in partners:
        pl.semaphore_signal(barrier, inc=1, device_id=partner, device_id_type=pl.DeviceIdType.MESH)

    depth_local = env.shape[0]
    bond, panel = Bond(here, bond_refs), Panel(here, panel_refs)
    height = bond.block.shape[2]

    def env_columns(i, slot):
        y, x = here.quarter(i)
        return pl.ds(pl.multiple_of((slot * 4 + y * 2 + x) * depth_local, 128), depth_local)

    def env_load(i, slot):
        at = (slice(None), env_columns(i, slot))
        return pltpu.make_async_copy(env_hbm.at[at], env.at[at], env_sem.at[i, slot])

    def site_load(phys):
        return pltpu.make_async_copy(site_hbm.at[phys], site.at[phys], site_sem.at[phys])

    for i in range(4):
        for slot in range(2):
            env_load(i, slot).start()
    for phys in range(PHYS):
        site_load(phys).start()

    exchange = send(window, windows, win_send, win_recv, here.at(col=1 - here.col))
    pl.semaphore_wait(barrier, len(partners))
    exchange.start()
    exchange.wait_recv()
    for phys in range(PHYS):
        flipped = (window[phys] + windows[phys]).T
        for k, z in enumerate(ORDER):
            at = phys * PANEL + k * height
            high, low = split(flipped[z * height : (z + 1) * height])
            pan[at : at + height, :] = high
            pan[PHYS * PANEL + at : PHYS * PANEL + at + height, :] = low

    def quarter_block(i):
        y, x = here.quarter(i)
        for slot in range(2):
            env_load(i, slot).wait()

        def one(slot, carry):
            product = dot3(pan[...], *split(env[:, env_columns(i, slot)]))
            product = product.reshape(PHYS, len(ORDER), height, depth_local)
            for phys in range(PHYS):
                for k in range(len(ORDER)):
                    bond.parts[phys, k, slot, y, x] = product[phys, k]
            return carry

        lax.fori_loop(0, 2, one, 0)

    step = 16

    def split_site(phys):
        site_load(phys).wait()

        def one(i, carry):
            at = pl.ds(pl.multiple_of(i * step, step), step)
            to = pl.ds(pl.multiple_of(phys * depth_local + i * step, step), step)
            high_site[to, :], low_site[to, :] = split(site[phys, at, :])
            return carry

        lax.fori_loop(0, depth_local // step, one, 0)

    def gather_block(g):
        bond.fetch(g)
        lhs[g] = jnp.concatenate(split(jnp.concatenate([bond.block[phys, g] for phys in range(PHYS)], axis=1)), axis=0)

    def panel_product(g, st, h):
        columns = panel.columns(st, h)
        panel.start(g, st, h, dot3(lhs[g], high_site[:, columns], low_site[:, columns]))

    run = {
        "Q": quarter_block,
        "W": split_site,
        "ZS": lambda k, h, i: bond.halve(h, k, i).start(),
        "ZB": lambda k, h: bond.add_pair(h, k, 1),
        "ZC": lambda k, h: bond.add_pair(h, k, 2),
        "SA": lambda k, h: bond.start(h, k),
        "F": lambda k, h: bond.forward(h, k),
        "C": lambda k, h: bond.finish_xy(h, k),
        "R": lambda k, h: bond.result(h, k),
        "D": gather_block,
        "PD": panel_product,
        "PF": panel.forward,
        "PC": panel.finish_xy,
        "PR": lambda g, st, h: panel.result(g, st, h, out),
    }
    for name, *at in STEPS:
        run[name](*at)

    exchange.wait_send()
    bond.drain()
    panel.drain()


def panel_window(site_tensors, panel_offset):
    cols_local = site_tensors.shape[2]
    padded = jnp.pad(site_tensors, ((0, 0), (0, 0), (PANEL, PANEL)))
    slice_start = jnp.clip(panel_offset[0] - lax.axis_index("col") * cols_local + PANEL, 0, cols_local + PANEL)
    return lax.dynamic_slice_in_dim(padded, slice_start, PANEL, 2)


def one_kernel(environment, site_tensors, panel_offset):
    depth_local, cols_local = environment.shape
    depth = len(ORDER)
    height = PANEL // depth
    any_space = pl.BlockSpec(memory_space=pl.ANY)
    in_vmem = pl.BlockSpec(memory_space=pltpu.VMEM)
    return pl.pallas_call(
        kernel,
        out_shape=jax.ShapeDtypeStruct((height // 4, cols_local), F32),
        in_specs=[in_vmem, any_space, any_space],
        out_specs=in_vmem,
        scratch_shapes=[
            pltpu.VMEM(environment.shape, F32),
            pltpu.VMEM(site_tensors.shape, F32),
            pltpu.VMEM((PHYS * depth_local, cols_local), BF16),
            pltpu.VMEM((PHYS * depth_local, cols_local), BF16),
            pltpu.VMEM((PHYS, depth_local, PANEL), F32),
            pltpu.VMEM((2 * PHYS * PANEL, depth_local), BF16),
            pltpu.VMEM((depth, 2 * height, PHYS * depth_local), BF16),
            pltpu.SemaphoreType.DMA((4, 2)),
            pltpu.SemaphoreType.DMA((PHYS,)),
            pltpu.SemaphoreType.DMA,
            pltpu.SemaphoreType.DMA,
        ]
        + Bond.scratch(depth, height, depth_local)
        + Panel.scratch(depth, height // 4, cols_local // (2 * STRIPES)),
        compiler_params=pltpu.CompilerParams(collective_id=0, has_side_effects=True, vmem_limit_bytes=50 * 1024 * 1024),
    )(panel_window(site_tensors, panel_offset), environment, site_tensors)


def collectives(environment, site_tensors, panel_offset):
    rows_local, cols_local = environment.shape
    col_index = lax.axis_index("col")
    panel_rows = lax.psum(panel_window(site_tensors, panel_offset), "col")
    first_col = lax.axis_index("row") * rows_local
    owner_col = first_col // cols_local
    owner_mask = (col_index == owner_col).astype(F32)
    accumulated = jnp.zeros((PANEL, cols_local), F32)
    for phys in range(PHYS):
        partial_one = jnp.dot(
            panel_rows[phys].T, environment, precision=lax.Precision.HIGHEST, preferred_element_type=F32
        )
        block_one = lax.dynamic_slice_in_dim(lax.psum(partial_one, "row"), first_col - owner_col * cols_local, rows_local, 1)
        fetched_one = lax.psum(block_one * owner_mask, "col")
        accumulated = accumulated + jnp.dot(
            fetched_one, site_tensors[phys], precision=lax.Precision.HIGHEST, preferred_element_type=F32
        )
    return lax.psum_scatter(accumulated, "row", scatter_dimension=0, tiled=True)


def solution(mesh):
    rows, cols = mesh.shape["row"], mesh.shape["col"]

    def shards(environment, site_tensors, panel_offset):
        depth_local, cols_local = environment.shape
        fits = (
            rows == 4 * len(ORDER)
            and cols == 2
            and depth_local % 128 == 0
            and cols_local == 8 * depth_local
            and cols_local % (2 * STRIPES * 128) == 0
            and PANEL % (8 * rows) == 0
        )
        if fits:
            return one_kernel(environment, site_tensors, panel_offset)
        return collectives(environment, site_tensors, panel_offset)

    return jax.shard_map(
        shards,
        mesh=mesh,
        in_specs=(P("row", "col"), P(None, "row", "col"), P()),
        out_specs=P("row", "col"),
        check_vma=False,
    )
```

```python
import functools

import jax
import jax.numpy as jnp
from jax import lax
from jax.experimental import pallas as pl
from jax.experimental.pallas import tpu as pltpu
from jax.sharding import PartitionSpec as P

PHYS = 2
PANEL = 128
STRIPES = 2
ORDER = (0, 3, 1, 2)
PAIRED = ((2, 0), (2, 1), (3, 0))
SLOTTED = ()
BOTH = -1
MIDDLE = ()
STEPS = (
    ("Q", 0, 0), ("Q", 0, 1), ("B",), ("SA", 0, 1, -1), ("ZS", 3, 0, 0), ("SA", 1, 0, -1), ("SA", 3, 1, -1), ("Q", 1, 0),
    ("Q", 1, 1), ("SA", 1, 1, -1), ("ZS", 2, 0, 1), ("SA", 0, 0, -1), ("Q", 2, 0), ("Q", 2, 1), ("ZS", 2, 0, 0), ("W", 0),
    ("ZS", 2, 1, 2), ("ZS", 2, 1, 1), ("Q", 3, 0), ("Q", 3, 1), ("F", 0, 1, -1), ("ZS", 2, 1, 0), ("ZS", 3, 0, 1),
    ("ZS", 2, 0, 3), ("SA", 3, 0, 0), ("ZS", 3, 0, 2), ("ZS", 3, 0, 3), ("F", 0, 0, -1), ("F", 1, 0, -1), ("ZB", 2, 0),
    ("ZC", 2, 1), ("C", 0, 1, -1), ("W", 1), ("ZS", 2, 0, 2), ("F", 1, 1, -1), ("SA", 2, 0, 0), ("C", 0, 0, -1), ("ZC", 3, 0),
    ("F", 3, 1, -1), ("C", 1, 0, -1), ("SA", 2, 1, 0), ("R", 0, 1), ("ZB", 3, 0), ("ZC", 2, 0), ("ZS", 2, 1, 3), ("C", 1, 1, -1),
    ("F", 3, 0, 0), ("R", 0, 0), ("F", 2, 0, 0), ("D", 0), ("PD", 0, 0, 0), ("C", 3, 1, -1), ("ZB", 2, 1), ("F", 2, 1, 0),
    ("PD", 0, 0, 1), ("PD", 0, 1, 0), ("PD", 0, 1, 1), ("R", 1, 0), ("C", 3, 0, 0), ("R", 1, 1), ("PF", 0, 0, 0), ("C", 2, 0, 0),
    ("D", 1), ("PD", 1, 0, 0), ("C", 2, 1, 0), ("PD", 1, 0, 1), ("R", 3, 1), ("PF", 0, 1, 0), ("PD", 1, 1, 0), ("PF", 0, 1, 1),
    ("R", 3, 0), ("PF", 0, 0, 1), ("PD", 1, 1, 1), ("PF", 1, 0, 0), ("R", 2, 0), ("D", 3), ("PD", 3, 0, 0), ("PC", 0, 0, 0),
    ("PF", 1, 0, 1), ("R", 2, 1), ("PD", 3, 0, 1), ("PC", 0, 1, 0), ("PD", 3, 1, 0), ("PF", 1, 1, 0), ("D", 2), ("PD", 2, 0, 0),
    ("PD", 2, 0, 1), ("PD", 3, 1, 1), ("PC", 1, 0, 0), ("PF", 1, 1, 1), ("PC", 0, 1, 1), ("PD", 2, 1, 0), ("PF", 3, 0, 1),
    ("PD", 2, 1, 1), ("PF", 3, 1, 0), ("PC", 0, 0, 1), ("PC", 1, 0, 1), ("PF", 2, 0, 1), ("PF", 2, 0, 0), ("PC", 1, 1, 0),
    ("PF", 2, 1, 0), ("PF", 3, 1, 1), ("PC", 1, 1, 1), ("PC", 3, 0, 1), ("PF", 2, 1, 1), ("PF", 3, 0, 0), ("PC", 3, 1, 0),
    ("PC", 2, 0, 1), ("PC", 2, 0, 0), ("PC", 2, 1, 0), ("PC", 3, 1, 1), ("PC", 2, 1, 1), ("PC", 3, 0, 0), ("E",), ("PR", 0, 1, 0),
    ("PR", 1, 0, 1), ("PR", 0, 0, 0), ("PR", 0, 1, 1), ("PR", 3, 1, 0), ("PR", 2, 0, 0), ("PR", 1, 0, 0), ("PR", 2, 0, 1),
    ("PR", 2, 1, 0), ("PR", 1, 1, 0), ("PR", 2, 1, 1), ("PR", 3, 1, 1), ("PR", 3, 0, 1), ("PR", 0, 0, 1), ("PR", 1, 1, 1),
    ("PR", 3, 0, 0),
)
F32 = jnp.float32
BF16 = jnp.bfloat16


def split(value):
    high = value.astype(BF16)
    return high, (value - high.astype(F32)).astype(BF16)


def dot3(lhs, rhs_high, rhs_low):
    count = lhs.shape[0] // 2
    dot = functools.partial(jnp.dot, preferred_element_type=F32)
    both = dot(lhs, rhs_high)
    return both[:count] + (both[count:] + dot(lhs[:count], rhs_low))


class Place:
    def __init__(self):
        row = lax.axis_index("row")
        self.col = lax.axis_index("col")
        self.x, self.y, self.z = row % 2, (row // 2) % 2, row // 4
        self.owner = self.z // 2 == self.col

    def at(self, x=None, y=None, z=None, col=None):
        x, y, z = (self.x if x is None else x), (self.y if y is None else y), (self.z if z is None else z)
        return (z * 4 + y * 2 + x, self.col if col is None else col)

    def quarter(self, i):
        return [(1 - self.y, 1 - self.x), (1 - self.y, self.x), (self.y, 1 - self.x), (self.y, self.x)][i]

    def first_link(self, half):
        return self.at(x=1 - self.x) if half == 0 else self.at(y=1 - self.y)

    def second_link(self, half):
        return self.at(y=1 - self.y) if half == 0 else self.at(x=1 - self.x)

    def passed(self, half):
        return self.quarter(1 if half == 0 else 2)

    def last(self, half):
        return self.quarter(2 if half == 0 else 1)


def send(src, dst, send_sem, recv_sem, device):
    return pltpu.make_async_remote_copy(
        src_ref=src, dst_ref=dst, send_sem=send_sem, recv_sem=recv_sem, device_id=device, device_id_type=pl.DeviceIdType.MESH
    )


class Bond:
    def __init__(self, place, refs, measure):
        self.place, self.measure = place, measure
        (self.parts, self.first, self.total, self.last_two, self.done, self.third, self.pair, self.block) = refs[:8]
        (self.first_recv, self.last_recv, self.z_recv, self.pair_recv, self.recv, self.sent) = refs[8:]
        self.kept = place.z % 2

    @staticmethod
    def pieces():
        units = [(h, k) for h in range(PHYS) for k in range(len(ORDER))]
        both = [u for u in units if (u[1], u[0]) in SLOTTED and (u[1], u[0]) not in PAIRED]
        return [(h, k, 0 if (k, h) in PAIRED else BOTH) for h, k in units if (h, k) not in both] + [
            (h, k, slot) for h, k in both for slot in range(2)
        ]

    @staticmethod
    def scratch(depth, height, width):
        pieces, pairs = len(Bond.pieces()), max(len(PAIRED), 1)
        return [
            pltpu.VMEM((PHYS, depth, 2, 2, 2, height, width), F32),
            pltpu.VMEM((PHYS, depth, 2, height, width), F32),
            pltpu.VMEM((PHYS, depth, 2, height, width), F32),
            pltpu.VMEM((PHYS, depth, 2, 2, height, width), F32),
            pltpu.VMEM((PHYS, depth, 2, height, width), F32),
            pltpu.VMEM((PHYS, depth, depth - 1, height, width), F32),
            pltpu.VMEM((pairs, 4, height, width), F32),
            pltpu.VMEM((depth, PHYS, height, width), F32),
        ] + [pltpu.SemaphoreType.DMA(shape) for shape in [(pieces,), (pieces,), (PHYS, depth), (pairs, 4), (depth,), (4,)]]

    def part(self, h, k, slot, at):
        y, x = at
        return (h, k, self.kept if (k, h) in PAIRED else self.span(slot), y, x)

    def span(self, slot):
        return slice(None) if slot == BOTH else slot

    def each(self, slot):
        return (0, 1) if slot == BOTH else (slot,)

    def hop(self, h, k, slot, n):
        here, i, span = self.place, self.pieces().index((h, k, slot)), self.span(slot)
        if n == 2:
            src, dst = self.total.at[h, k, span], self.last_two.at[h, k, 1, span]
            return send(src, dst, self.sent.at[0], self.last_recv.at[i], here.second_link(h))
        src = self.parts.at[self.part(h, k, slot, here.quarter(0) if n == 0 else here.last(h))]
        if n == 0:
            return send(src, self.first.at[h, k, span], self.sent.at[0], self.first_recv.at[i], here.first_link(h))
        return send(src, self.last_two.at[h, k, 0, span], self.sent.at[0], self.last_recv.at[i], here.first_link(h))

    def both_last(self, h, k, slot):
        ref = self.last_two.at[h, k, :, self.span(slot)]
        return send(ref, ref, self.sent.at[0], self.last_recv.at[self.pieces().index((h, k, slot))], self.place.first_link(h))

    def halve(self, h, k, i):
        here, n = self.place, PAIRED.index((k, h))
        y, x = here.quarter(i)
        partner = here.at(z=here.z + 1 - 2 * self.kept)
        return send(
            self.parts.at[h, k, 1 - self.kept, y, x], self.pair.at[n, i], self.sent.at[1], self.pair_recv.at[n, i], partner
        )

    def add_pair(self, h, k, i):
        self.halve(h, k, i).wait_recv()
        at = self.part(h, k, 0, self.place.quarter(i))
        self.parts[at] = self.parts[at] + self.pair[PAIRED.index((k, h)), i]

    def plane(self, h, k, slot):
        return self.place.col * 2 + (self.kept if (k, h) in PAIRED else slot)

    def across(self, h, k, slot):
        here, z = self.place, self.plane(h, k, slot)
        landing = 1 if (k, h) in PAIRED else (here.z - z + 3) % 4
        return send(self.done.at[h, k, slot], self.third.at[h, k, landing], self.sent.at[2], self.z_recv.at[h, k], here.at(z=z))

    def arrivals(self, h, k):
        ref = self.third.at[h, k, 1] if (k, h) in PAIRED else self.third.at[h, k]
        return send(ref, ref, self.sent.at[2], self.z_recv.at[h, k], self.place.at(z=(self.place.z + 2) % 4))

    def share(self, h, k):
        here, ref = self.place, self.block.at[k, h]
        return send(ref, ref, self.sent.at[3], self.recv.at[k], here.at(col=1 - here.col))

    def start(self, h, k, slot):
        if (k, h) in PAIRED:
            self.add_pair(h, k, 0)
        self.hop(h, k, slot, 0).start()

    def forward(self, h, k, slot):
        self.hop(h, k, slot, 0).wait_recv()
        for one in self.each(slot):
            self.total[h, k, one] = self.parts[self.part(h, k, one, self.place.passed(h))] + self.first[h, k, one]
        self.hop(h, k, slot, 2).start()
        self.hop(h, k, slot, 1).start()

    def finish_xy(self, h, k, slot):
        if (k, h) in PAIRED:
            self.add_pair(h, k, 3)
        self.both_last(h, k, slot).wait_recv()
        for one in self.each(slot):
            mine = self.parts[self.part(h, k, one, self.place.quarter(3))]
            self.done[h, k, one] = (mine + self.last_two[h, k, 0, one]) + self.last_two[h, k, 1, one]
        for one in self.each(slot):

            @pl.when(self.plane(h, k, one) != self.place.z)
            def _():
                self.across(h, k, one).start()

    def result(self, h, k):
        @pl.when(self.place.owner)
        def _():
            self.arrivals(h, k).wait_recv()
            if (k, h) in PAIRED:
                value = self.done[h, k, 0] + self.third[h, k, 1]
            else:
                value = self.done[h, k, self.kept]
                for j in (0, 2, 1):
                    value = value + self.third[h, k, j]
            self.block[k, h] = value
            self.share(h, k).start()

    def fetch(self, k):
        @pl.when(jnp.logical_not(self.place.owner))
        def _():
            here, ref = self.place, self.block.at[k]
            send(ref, ref, self.sent.at[3], self.recv.at[k], here.at(col=1 - here.col)).wait_recv()

    def sent_bytes(self, n, count):
        ref = self.measure.at[pl.ds(0, 8 * count), pl.ds(0, self.block.shape[2] * self.block.shape[3] // 8)]
        send(ref, ref, self.sent.at[n], self.recv.at[0], self.place.at(col=1 - self.place.col)).wait_send()

    def drain(self):
        units, pairs = PHYS * len(ORDER), len(PAIRED)
        self.sent_bytes(0, 6 * (units - pairs) + 3 * pairs)
        if pairs:
            self.sent_bytes(1, 4 * pairs)

        @pl.when(self.place.owner)
        def _():
            self.sent_bytes(2, units - pairs)
            self.sent_bytes(3, units)

        @pl.when(jnp.logical_not(self.place.owner))
        def _():
            self.sent_bytes(2, 2 * (units - pairs) + pairs)


class Panel:
    def __init__(self, place, refs, measure):
        self.place, self.measure = place, measure
        self.parts, self.first, self.total, self.last_two, self.done, self.third, self.pair, self.pair_third = refs[:8]
        self.first_recv, self.last_recv, self.z_recv, self.sent = refs[8:]
        self.width = self.parts.shape[-1]

    @staticmethod
    def scratch(depth, height, width):
        one = pltpu.VMEM((depth, 2, STRIPES, height, width), F32)
        two = pltpu.VMEM((depth, 2, STRIPES, 2, height, width), F32)
        return [
            pltpu.VMEM((depth, 2, STRIPES, 2, 2, height, width), F32),
            two,
            one,
            two,
            one,
            pltpu.VMEM((2, STRIPES, depth - 1, height, width), F32),
            two,
            pltpu.VMEM((2, STRIPES, depth - 1, 2, height, width), F32),
        ] + [
            pltpu.SemaphoreType.DMA(shape)
            for shape in [(depth, 2, STRIPES), (depth, 2, STRIPES), (2, STRIPES), (2,)]
        ]

    def columns(self, st, h):
        return pl.ds((h * STRIPES + st) * self.width, self.width)

    def hop(self, g, st, h, n):
        here = self.place
        if n == 2:
            dst, recv = self.last_two.at[g, h, st, 1], self.last_recv.at[g, h, st]
            return send(self.total.at[g, h, st], dst, self.sent.at[0], recv, here.second_link(h))
        y, x = here.quarter(0) if n == 0 else here.last(h)
        dst, recv = (self.first, self.first_recv) if n == 0 else (self.last_two, self.last_recv)
        src, dst = self.parts.at[g, h, st, y, x], dst.at[g, h, st, 0]
        return send(src, dst, self.sent.at[0], recv.at[g, h, st], here.first_link(h))

    def both_last(self, g, st, h):
        ref = self.last_two.at[g, h, st]
        return send(ref, ref, self.sent.at[0], self.last_recv.at[g, h, st], self.place.first_link(h))

    def landing(self, g):
        return (self.place.z - ORDER[g] + 3) % 4

    def across(self, g, st, h):
        dst = self.third.at[h, st, self.landing(g)]
        return send(self.done.at[g, h, st], dst, self.sent.at[1], self.z_recv.at[h, st], self.place.at(z=ORDER[g]))

    def arrivals(self, g, st, h):
        ref = (self.pair_third if (g, st, h) in MIDDLE else self.third).at[h, st]
        return send(ref, ref, self.sent.at[1], self.z_recv.at[h, st], self.place.at(z=(self.place.z + 1) % 4))

    def half_pair(self, h):
        here = self.place
        return (slice(None), 1 - here.x) if h == 0 else (1 - here.y, slice(None))

    def inner(self, h):
        return self.place.y if h == 0 else self.place.x

    def pair_hop(self, g, st, h):
        src = self.parts.at[(g, h, st, *self.half_pair(h))]
        return send(src, self.first.at[g, h, st], self.sent.at[0], self.first_recv.at[g, h, st], self.place.first_link(h))

    def pair_across(self, g, st, h):
        dst = self.pair_third.at[h, st, self.landing(g)]
        return send(self.pair.at[g, h, st], dst, self.sent.at[1], self.z_recv.at[h, st], self.place.at(z=ORDER[g]))

    def last_hop(self, g, st, h):
        src, dst = self.pair.at[g, h, st, 1 - self.inner(h)], self.last_two.at[g, h, st, 1]
        return send(src, dst, self.sent.at[0], self.last_recv.at[g, h, st], self.place.second_link(h))

    def start(self, g, st, h, product):
        self.parts[g, h, st] = product.reshape(self.parts.shape[3:])
        if (g, st, h) in MIDDLE:
            self.pair_hop(g, st, h).start()
        else:
            self.hop(g, st, h, 0).start()

    def forward(self, g, st, h):
        here = self.place
        if (g, st, h) in MIDDLE:
            self.pair_hop(g, st, h).wait_recv()
            for i in range(2):
                y, x = (i, here.x) if h == 0 else (here.y, i)
                self.pair[g, h, st, i] = self.parts[g, h, st, y, x] + self.first[g, h, st, i]

            @pl.when(here.z != ORDER[g])
            def _():
                self.pair_across(g, st, h).start()

            return
        y, x = here.passed(h)
        self.hop(g, st, h, 0).wait_recv()
        self.total[g, h, st] = self.parts[g, h, st, y, x] + self.first[g, h, st, 0]
        self.hop(g, st, h, 2).start()
        self.hop(g, st, h, 1).start()

    def finish_xy(self, g, st, h):
        here = self.place
        if (g, st, h) in MIDDLE:

            @pl.when(here.z == ORDER[g])
            def _():
                self.arrivals(g, st, h).wait_recv()
                value = self.pair[g, h, st]
                for j in (0, 2, 1):
                    value = value + self.pair_third[h, st, j]
                self.pair[g, h, st] = value
                self.last_hop(g, st, h).start()

            return
        y, x = here.quarter(3)
        self.both_last(g, st, h).wait_recv()
        self.done[g, h, st] = (self.parts[g, h, st, y, x] + self.last_two[g, h, st, 0]) + self.last_two[g, h, st, 1]

        @pl.when(here.z != ORDER[g])
        def _():
            self.across(g, st, h).start()

    def result(self, g, st, h, out):
        here = self.place

        @pl.when(here.z == ORDER[g])
        def _():
            if (g, st, h) in MIDDLE:
                self.last_hop(g, st, h).wait_recv()
                out[:, self.columns(st, h)] = self.pair[g, h, st, self.inner(h)] + self.last_two[g, h, st, 1]
                return
            self.arrivals(g, st, h).wait_recv()
            value = self.done[g, h, st]
            for j in (0, 2, 1):
                value = value + self.third[h, st, j]
            out[:, self.columns(st, h)] = value

    def drain(self):
        here = self.place
        units = [(g, st, h) for g in range(len(ORDER)) for st in range(STRIPES) for h in range(2)]

        def sent_bytes(n, count):
            ref = self.measure.at[pl.ds(0, self.parts.shape[-2] * count), pl.ds(0, self.width)]
            send(ref, ref, self.sent.at[n], self.first_recv.at[0, 0, 0], here.at(col=1 - here.col)).wait_send()

        for own, z in enumerate(ORDER):

            @pl.when(here.z == z)
            def _():
                sent_bytes(0, sum(3 if u not in MIDDLE else 3 if u[0] == own else 2 for u in units))
                sent_bytes(1, sum(2 if u in MIDDLE else 1 for u in units if u[0] != own))


def kernel(window, env_hbm, site_hbm, out, env, site, high_site, low_site, windows, pan, lhs, *rest):
    env_sem, site_sem, win_send, win_recv, ready = rest[:5]
    bond_refs, panel_refs = rest[5:19], rest[19:31]
    here = Place()
    barrier = pltpu.get_barrier_semaphore()
    chips = [here.at(x=1 - here.x, col=0), here.at(y=1 - here.y, col=0)]
    chips += [here.at(z=(here.z + j) % 4, col=0) for j in range(1, 4)]
    first = here.col == 0
    second = jnp.logical_not(first)

    def signal(semaphore, device):
        pl.semaphore_signal(semaphore, inc=1, device_id=device, device_id_type=pl.DeviceIdType.MESH)

    @pl.when(first)
    def _():
        signal(barrier, here.at(col=1))

    for chip in chips:
        signal(barrier, chip)

    depth_local = env.shape[0]
    bond, panel = Bond(here, bond_refs, env), Panel(here, panel_refs, env)
    height = bond.block.shape[2]

    def env_columns(i, slot):
        y, x = here.quarter(i)
        return pl.ds(pl.multiple_of((slot * 4 + y * 2 + x) * depth_local, 128), depth_local)

    def env_load(i, slot):
        at = (slice(None), env_columns(i, slot))
        return pltpu.make_async_copy(env_hbm.at[at], env.at[at], env_sem.at[i, slot])

    def site_load(phys):
        return pltpu.make_async_copy(site_hbm.at[phys], site.at[phys], site_sem.at[phys])

    for i in range(4):
        for slot in range(2):
            env_load(i, slot).start()
    for phys in range(PHYS):
        site_load(phys).start()

    exchange = send(window, windows, win_send, win_recv, here.at(col=1 - here.col))

    @pl.when(second)
    def _():
        pl.semaphore_wait(barrier, 1)
        signal(ready, here.at(col=0))

    @pl.when(first)
    def _():
        pl.semaphore_wait(ready, 1)

    exchange.start()
    exchange.wait_recv()
    for phys in range(PHYS):
        flipped = (window[phys] + windows[phys]).T
        for k, z in enumerate(ORDER):
            at = phys * PANEL + k * height
            high, low = split(flipped[z * height : (z + 1) * height])
            pan[at : at + height, :] = high
            pan[PHYS * PANEL + at : PHYS * PANEL + at + height, :] = low

    def quarter_block(i, slot):
        y, x = here.quarter(i)
        env_load(i, slot).wait()
        product = dot3(pan[...], *split(env[:, env_columns(i, slot)]))
        product = product.reshape(PHYS, len(ORDER), height, depth_local)
        for phys in range(PHYS):
            for k in range(len(ORDER)):
                bond.parts[phys, k, slot, y, x] = product[phys, k]

    step = 16

    def split_site(phys):
        site_load(phys).wait()

        def one(i, carry):
            at = pl.ds(pl.multiple_of(i * step, step), step)
            to = pl.ds(pl.multiple_of(phys * depth_local + i * step, step), step)
            high_site[to, :], low_site[to, :] = split(site[phys, at, :])
            return carry

        lax.fori_loop(0, depth_local // step, one, 0)

    def gather_block(g):
        bond.fetch(g)
        lhs[g] = jnp.concatenate(split(jnp.concatenate([bond.block[g, phys] for phys in range(PHYS)], axis=1)), axis=0)

    def panel_product(g, st, h):
        columns = panel.columns(st, h)
        panel.start(g, st, h, dot3(lhs[g], high_site[:, columns], low_site[:, columns]))

    def greet():
        @pl.when(first)
        def _():
            pl.semaphore_wait(barrier, 2 * len(chips))
            signal(ready, here.at(col=1))

        @pl.when(second)
        def _():
            pl.semaphore_wait(ready, 1)

    def drain():
        exchange.wait_send()
        bond.drain()
        panel.drain()

    run = {
        "B": greet,
        "E": drain,
        "Q": quarter_block,
        "W": split_site,
        "ZS": lambda k, h, i: bond.halve(h, k, i).start(),
        "ZB": lambda k, h: bond.add_pair(h, k, 1),
        "ZC": lambda k, h: bond.add_pair(h, k, 2),
        "SA": lambda k, h, slot: bond.start(h, k, slot),
        "F": lambda k, h, slot: bond.forward(h, k, slot),
        "C": lambda k, h, slot: bond.finish_xy(h, k, slot),
        "R": lambda k, h: bond.result(h, k),
        "D": gather_block,
        "PD": panel_product,
        "PF": panel.forward,
        "PC": panel.finish_xy,
        "PR": lambda g, st, h: panel.result(g, st, h, out),
    }
    for name, *at in STEPS:
        run[name](*at)


def panel_window(site_tensors, panel_offset):
    cols_local = site_tensors.shape[2]
    padded = jnp.pad(site_tensors, ((0, 0), (0, 0), (PANEL, PANEL)))
    slice_start = jnp.clip(panel_offset[0] - lax.axis_index("col") * cols_local + PANEL, 0, cols_local + PANEL)
    return lax.dynamic_slice_in_dim(padded, slice_start, PANEL, 2)


def one_kernel(environment, site_tensors, panel_offset):
    depth_local, cols_local = environment.shape
    depth = len(ORDER)
    height = PANEL // depth
    any_space = pl.BlockSpec(memory_space=pl.ANY)
    in_vmem = pl.BlockSpec(memory_space=pltpu.VMEM)
    return pl.pallas_call(
        kernel,
        out_shape=jax.ShapeDtypeStruct((height // 4, cols_local), F32),
        in_specs=[in_vmem, any_space, any_space],
        out_specs=in_vmem,
        scratch_shapes=[
            pltpu.VMEM(environment.shape, F32),
            pltpu.VMEM(site_tensors.shape, F32),
            pltpu.VMEM((PHYS * depth_local, cols_local), BF16),
            pltpu.VMEM((PHYS * depth_local, cols_local), BF16),
            pltpu.VMEM((PHYS, depth_local, PANEL), F32),
            pltpu.VMEM((2 * PHYS * PANEL, depth_local), BF16),
            pltpu.VMEM((depth, 2 * height, PHYS * depth_local), BF16),
            pltpu.SemaphoreType.DMA((4, 2)),
            pltpu.SemaphoreType.DMA((PHYS,)),
            pltpu.SemaphoreType.DMA,
            pltpu.SemaphoreType.DMA,
            pltpu.SemaphoreType.REGULAR,
        ]
        + Bond.scratch(depth, height, depth_local)
        + Panel.scratch(depth, height // 4, cols_local // (2 * STRIPES)),
        compiler_params=pltpu.CompilerParams(collective_id=0, has_side_effects=True, vmem_limit_bytes=50 * 1024 * 1024),
    )(panel_window(site_tensors, panel_offset), environment, site_tensors)


def collectives(environment, site_tensors, panel_offset):
    rows_local, cols_local = environment.shape
    col_index = lax.axis_index("col")
    panel_rows = lax.psum(panel_window(site_tensors, panel_offset), "col")
    first_col = lax.axis_index("row") * rows_local
    owner_col = first_col // cols_local
    owner_mask = (col_index == owner_col).astype(F32)
    accumulated = jnp.zeros((PANEL, cols_local), F32)
    for phys in range(PHYS):
        partial_one = jnp.dot(
            panel_rows[phys].T, environment, precision=lax.Precision.HIGHEST, preferred_element_type=F32
        )
        block_one = lax.dynamic_slice_in_dim(lax.psum(partial_one, "row"), first_col - owner_col * cols_local, rows_local, 1)
        fetched_one = lax.psum(block_one * owner_mask, "col")
        accumulated = accumulated + jnp.dot(
            fetched_one, site_tensors[phys], precision=lax.Precision.HIGHEST, preferred_element_type=F32
        )
    return lax.psum_scatter(accumulated, "row", scatter_dimension=0, tiled=True)


def solution(mesh):
    rows, cols = mesh.shape["row"], mesh.shape["col"]

    def shards(environment, site_tensors, panel_offset):
        depth_local, cols_local = environment.shape
        fits = (
            rows == 4 * len(ORDER)
            and cols == 2
            and depth_local % 128 == 0
            and cols_local == 8 * depth_local
            and cols_local % (2 * STRIPES * 128) == 0
            and depth_local >= 8 * 6 * PHYS * len(ORDER)
            and depth_local >= 8 * 12 * STRIPES * 2
            and PANEL % (8 * rows) == 0
        )
        if fits:
            return one_kernel(environment, site_tensors, panel_offset)
        return collectives(environment, site_tensors, panel_offset)

    return jax.shard_map(
        shards,
        mesh=mesh,
        in_specs=(P("row", "col"), P(None, "row", "col"), P()),
        out_specs=P("row", "col"),
        check_vma=False,
    )
```

```python
import functools

import jax
import jax.numpy as jnp
from jax import lax
from jax.experimental import pallas as pl
from jax.experimental.pallas import tpu as pltpu
from jax.sharding import PartitionSpec as P

PHYS = 2
PANEL = 128
STRIPES = 2
ORDER = (0, 3, 1, 2)
PAIRED = ((2, 0), (3, 0), (3, 1))
SLOTTED = ((0, 0), (0, 1), (1, 0), (1, 1), (2, 0), (2, 1), (3, 0), (3, 1))
BOTH = -1
MIDDLE = ()
STEPS = (
    ("Q", 0, 0), ("B",), ("SA", 0, 1, 0), ("SA", 0, 0, 0), ("Q", 0, 1), ("ZS", 2, 0, 0), ("SA", 1, 1, 0), ("ZS", 3, 1, 0),
    ("Q", 1, 0), ("Q", 1, 1), ("SA", 1, 0, 1), ("ZS", 2, 0, 1), ("Q", 2, 0), ("ZS", 3, 0, 1), ("SA", 0, 1, 1), ("Q", 2, 1),
    ("SA", 1, 1, 1), ("SA", 1, 0, 0), ("SA", 0, 0, 1), ("W", 1), ("ZS", 3, 1, 1), ("F", 0, 1, 0), ("ZS", 3, 0, 0), ("F", 0, 0, 0),
    ("ZS", 2, 0, 2), ("Q", 3, 0), ("ZS", 3, 0, 2), ("W", 0), ("ZS", 3, 1, 2), ("F", 1, 0, 1), ("F", 0, 0, 1), ("Q", 3, 1),
    ("ZB", 2, 0), ("F", 0, 1, 1), ("SA", 2, 1, 1), ("C", 0, 0, 0), ("SA", 2, 0, 0), ("ZB", 3, 0), ("C", 1, 0, 1), ("SA", 2, 1, 0),
    ("F", 1, 0, 0), ("C", 0, 0, 1), ("F", 1, 1, 1), ("C", 0, 1, 1), ("F", 1, 1, 0), ("SA", 3, 1, 0), ("C", 0, 1, 0), ("ZC", 2, 0),
    ("SA", 3, 0, 0), ("F", 2, 0, 0), ("ZS", 2, 0, 3), ("F", 2, 1, 1), ("C", 1, 0, 0), ("ZS", 3, 1, 3), ("R", 0, 0),
    ("C", 1, 1, 1), ("C", 1, 1, 0), ("ZC", 3, 1), ("ZB", 3, 1), ("F", 2, 1, 0), ("F", 3, 1, 0), ("R", 0, 1), ("C", 2, 0, 0),
    ("ZC", 3, 0), ("ZS", 3, 0, 3), ("F", 3, 0, 0), ("D", 0), ("PD", 0, 0, 0), ("PD", 0, 0, 1), ("C", 2, 1, 1), ("PD", 0, 1, 0),
    ("R", 1, 0), ("C", 2, 1, 0), ("R", 1, 1), ("PD", 0, 1, 1), ("D", 1), ("C", 3, 1, 0), ("PD", 1, 0, 0), ("C", 3, 0, 0),
    ("R", 2, 0), ("PF", 0, 0, 0), ("PD", 1, 0, 1), ("PF", 0, 1, 0), ("PD", 1, 1, 0), ("PD", 1, 1, 1), ("PF", 0, 1, 1),
    ("PF", 0, 0, 1), ("R", 2, 1), ("PF", 1, 0, 0), ("R", 3, 1), ("D", 2), ("PD", 2, 0, 0), ("PD", 2, 0, 1), ("PF", 1, 0, 1),
    ("R", 3, 0), ("PD", 2, 1, 0), ("PD", 2, 1, 1), ("PF", 1, 1, 1), ("PC", 0, 0, 0), ("D", 3), ("PC", 0, 1, 1), ("PD", 3, 0, 0),
    ("PF", 1, 1, 0), ("PD", 3, 0, 1), ("PD", 3, 1, 0), ("PC", 0, 1, 0), ("PF", 2, 0, 0), ("PC", 1, 0, 0), ("PD", 3, 1, 1),
    ("PF", 2, 0, 1), ("PF", 2, 1, 0), ("PC", 0, 0, 1), ("PC", 1, 1, 1), ("PC", 1, 0, 1), ("PF", 3, 0, 0), ("PC", 1, 1, 0),
    ("PF", 3, 0, 1), ("PF", 3, 1, 0), ("PC", 2, 0, 1), ("PF", 2, 1, 1), ("PC", 2, 1, 0), ("PF", 3, 1, 1), ("PC", 3, 0, 0),
    ("PC", 3, 0, 1), ("PC", 2, 0, 0), ("PC", 3, 1, 0), ("PC", 2, 1, 1), ("PC", 3, 1, 1), ("E",), ("PR", 1, 0, 0), ("PR", 1, 1, 1),
    ("PR", 2, 0, 0), ("PR", 3, 0, 1), ("PR", 3, 1, 0), ("PR", 2, 1, 1), ("PR", 0, 0, 0), ("PR", 1, 1, 0), ("PR", 3, 0, 0),
    ("PR", 0, 0, 1), ("PR", 3, 1, 1), ("PR", 2, 0, 1), ("PR", 0, 1, 0), ("PR", 1, 0, 1), ("PR", 0, 1, 1), ("PR", 2, 1, 0),
)
F32 = jnp.float32
BF16 = jnp.bfloat16


def split(value):
    high = value.astype(BF16)
    return high, (value - high.astype(F32)).astype(BF16)


def dot3(lhs, rhs_high, rhs_low):
    count = lhs.shape[0] // 2
    dot = functools.partial(jnp.dot, preferred_element_type=F32)
    both = dot(lhs, rhs_high)
    return both[:count] + (both[count:] + dot(lhs[:count], rhs_low))


class Place:
    def __init__(self):
        row = lax.axis_index("row")
        self.col = lax.axis_index("col")
        self.x, self.y, self.z = row % 2, (row // 2) % 2, row // 4
        self.owner = self.z // 2 == self.col

    def at(self, x=None, y=None, z=None, col=None):
        x, y, z = (self.x if x is None else x), (self.y if y is None else y), (self.z if z is None else z)
        return (z * 4 + y * 2 + x, self.col if col is None else col)

    def quarter(self, i):
        return [(1 - self.y, 1 - self.x), (1 - self.y, self.x), (self.y, 1 - self.x), (self.y, self.x)][i]

    def first_link(self, half):
        return self.at(x=1 - self.x) if half == 0 else self.at(y=1 - self.y)

    def second_link(self, half):
        return self.at(y=1 - self.y) if half == 0 else self.at(x=1 - self.x)

    def passed(self, half):
        return self.quarter(1 if half == 0 else 2)

    def last(self, half):
        return self.quarter(2 if half == 0 else 1)


def send(src, dst, send_sem, recv_sem, device):
    return pltpu.make_async_remote_copy(
        src_ref=src, dst_ref=dst, send_sem=send_sem, recv_sem=recv_sem, device_id=device, device_id_type=pl.DeviceIdType.MESH
    )


class Bond:
    def __init__(self, place, refs, measure):
        self.place, self.measure = place, measure
        (self.parts, self.first, self.total, self.last_two, self.done, self.third, self.pair, self.block) = refs[:8]
        (self.first_recv, self.last_recv, self.z_recv, self.pair_recv, self.recv, self.sent) = refs[8:]
        self.kept = place.z % 2

    @staticmethod
    def pieces():
        units = [(h, k) for h in range(PHYS) for k in range(len(ORDER))]
        both = [u for u in units if (u[1], u[0]) in SLOTTED and (u[1], u[0]) not in PAIRED]
        return [(h, k, 0 if (k, h) in PAIRED else BOTH) for h, k in units if (h, k) not in both] + [
            (h, k, slot) for h, k in both for slot in range(2)
        ]

    @staticmethod
    def scratch(depth, height, width):
        pieces, pairs = len(Bond.pieces()), max(len(PAIRED), 1)
        return [
            pltpu.VMEM((PHYS, depth, 2, 2, 2, height, width), F32),
            pltpu.VMEM((PHYS, depth, 2, height, width), F32),
            pltpu.VMEM((PHYS, depth, 2, height, width), F32),
            pltpu.VMEM((PHYS, depth, 2, 2, height, width), F32),
            pltpu.VMEM((PHYS, depth, 2, height, width), F32),
            pltpu.VMEM((PHYS, depth, depth - 1, height, width), F32),
            pltpu.VMEM((pairs, 4, height, width), F32),
            pltpu.VMEM((depth, PHYS, height, width), F32),
        ] + [pltpu.SemaphoreType.DMA(shape) for shape in [(pieces,), (pieces,), (PHYS, depth), (pairs, 4), (depth,), (4,)]]

    def part(self, h, k, slot, at):
        y, x = at
        return (h, k, self.kept if (k, h) in PAIRED else self.span(slot), y, x)

    def span(self, slot):
        return slice(None) if slot == BOTH else slot

    def each(self, slot):
        return (0, 1) if slot == BOTH else (slot,)

    def hop(self, h, k, slot, n):
        here, i, span = self.place, self.pieces().index((h, k, slot)), self.span(slot)
        if n == 2:
            src, dst = self.total.at[h, k, span], self.last_two.at[h, k, 1, span]
            return send(src, dst, self.sent.at[0], self.last_recv.at[i], here.second_link(h))
        src = self.parts.at[self.part(h, k, slot, here.quarter(0) if n == 0 else here.last(h))]
        if n == 0:
            return send(src, self.first.at[h, k, span], self.sent.at[0], self.first_recv.at[i], here.first_link(h))
        return send(src, self.last_two.at[h, k, 0, span], self.sent.at[0], self.last_recv.at[i], here.first_link(h))

    def both_last(self, h, k, slot):
        ref = self.last_two.at[h, k, :, self.span(slot)]
        return send(ref, ref, self.sent.at[0], self.last_recv.at[self.pieces().index((h, k, slot))], self.place.first_link(h))

    def halve(self, h, k, i):
        here, n = self.place, PAIRED.index((k, h))
        y, x = here.quarter(i)
        partner = here.at(z=here.z + 1 - 2 * self.kept)
        return send(
            self.parts.at[h, k, 1 - self.kept, y, x], self.pair.at[n, i], self.sent.at[1], self.pair_recv.at[n, i], partner
        )

    def add_pair(self, h, k, i):
        self.halve(h, k, i).wait_recv()
        at = self.part(h, k, 0, self.place.quarter(i))
        self.parts[at] = self.parts[at] + self.pair[PAIRED.index((k, h)), i]

    def plane(self, h, k, slot):
        return self.place.col * 2 + (self.kept if (k, h) in PAIRED else slot)

    def across(self, h, k, slot):
        here, z = self.place, self.plane(h, k, slot)
        landing = 1 if (k, h) in PAIRED else (here.z - z + 3) % 4
        return send(self.done.at[h, k, slot], self.third.at[h, k, landing], self.sent.at[2], self.z_recv.at[h, k], here.at(z=z))

    def arrivals(self, h, k):
        ref = self.third.at[h, k, 1] if (k, h) in PAIRED else self.third.at[h, k]
        return send(ref, ref, self.sent.at[2], self.z_recv.at[h, k], self.place.at(z=(self.place.z + 2) % 4))

    def share(self, h, k):
        here, ref = self.place, self.block.at[k, h]
        return send(ref, ref, self.sent.at[3], self.recv.at[k], here.at(col=1 - here.col))

    def start(self, h, k, slot):
        if (k, h) in PAIRED:
            self.add_pair(h, k, 0)
        self.hop(h, k, slot, 0).start()

    def forward(self, h, k, slot):
        self.hop(h, k, slot, 0).wait_recv()
        for one in self.each(slot):
            self.total[h, k, one] = self.parts[self.part(h, k, one, self.place.passed(h))] + self.first[h, k, one]
        self.hop(h, k, slot, 2).start()
        self.hop(h, k, slot, 1).start()

    def finish_xy(self, h, k, slot):
        if (k, h) in PAIRED:
            self.add_pair(h, k, 3)
        self.both_last(h, k, slot).wait_recv()
        for one in self.each(slot):
            mine = self.parts[self.part(h, k, one, self.place.quarter(3))]
            self.done[h, k, one] = (mine + self.last_two[h, k, 0, one]) + self.last_two[h, k, 1, one]
        for one in self.each(slot):

            @pl.when(self.plane(h, k, one) != self.place.z)
            def _():
                self.across(h, k, one).start()

    def result(self, h, k):
        @pl.when(self.place.owner)
        def _():
            self.arrivals(h, k).wait_recv()
            if (k, h) in PAIRED:
                value = self.done[h, k, 0] + self.third[h, k, 1]
            else:
                value = self.done[h, k, self.kept]
                for j in (0, 2, 1):
                    value = value + self.third[h, k, j]
            self.block[k, h] = value
            self.share(h, k).start()

    def fetch(self, k):
        @pl.when(jnp.logical_not(self.place.owner))
        def _():
            here, ref = self.place, self.block.at[k]
            send(ref, ref, self.sent.at[3], self.recv.at[k], here.at(col=1 - here.col)).wait_recv()

    def sent_bytes(self, n, count):
        ref = self.measure.at[pl.ds(0, 8 * count), pl.ds(0, self.block.shape[2] * self.block.shape[3] // 8)]
        send(ref, ref, self.sent.at[n], self.recv.at[0], self.place.at(col=1 - self.place.col)).wait_send()

    def drain(self):
        units, pairs = PHYS * len(ORDER), len(PAIRED)
        self.sent_bytes(0, 6 * (units - pairs) + 3 * pairs)
        if pairs:
            self.sent_bytes(1, 4 * pairs)

        @pl.when(self.place.owner)
        def _():
            self.sent_bytes(2, units - pairs)
            self.sent_bytes(3, units)

        @pl.when(jnp.logical_not(self.place.owner))
        def _():
            self.sent_bytes(2, 2 * (units - pairs) + pairs)


class Panel:
    def __init__(self, place, refs, measure):
        self.place, self.measure = place, measure
        self.parts, self.first, self.total, self.last_two, self.done, self.third, self.pair, self.pair_third = refs[:8]
        self.first_recv, self.last_recv, self.z_recv, self.sent = refs[8:]
        self.width = self.parts.shape[-1]

    @staticmethod
    def scratch(depth, height, width):
        one = pltpu.VMEM((depth, 2, STRIPES, height, width), F32)
        two = pltpu.VMEM((depth, 2, STRIPES, 2, height, width), F32)
        return [
            pltpu.VMEM((depth, 2, STRIPES, 2, 2, height, width), F32),
            two,
            one,
            two,
            one,
            pltpu.VMEM((2, STRIPES, depth - 1, height, width), F32),
            two,
            pltpu.VMEM((2, STRIPES, depth - 1, 2, height, width), F32),
        ] + [
            pltpu.SemaphoreType.DMA(shape)
            for shape in [(depth, 2, STRIPES), (depth, 2, STRIPES), (2, STRIPES), (2,)]
        ]

    def columns(self, st, h):
        return pl.ds((h * STRIPES + st) * self.width, self.width)

    def hop(self, g, st, h, n):
        here = self.place
        if n == 2:
            dst, recv = self.last_two.at[g, h, st, 1], self.last_recv.at[g, h, st]
            return send(self.total.at[g, h, st], dst, self.sent.at[0], recv, here.second_link(h))
        y, x = here.quarter(0) if n == 0 else here.last(h)
        dst, recv = (self.first, self.first_recv) if n == 0 else (self.last_two, self.last_recv)
        src, dst = self.parts.at[g, h, st, y, x], dst.at[g, h, st, 0]
        return send(src, dst, self.sent.at[0], recv.at[g, h, st], here.first_link(h))

    def both_last(self, g, st, h):
        ref = self.last_two.at[g, h, st]
        return send(ref, ref, self.sent.at[0], self.last_recv.at[g, h, st], self.place.first_link(h))

    def landing(self, g):
        return (self.place.z - ORDER[g] + 3) % 4

    def across(self, g, st, h):
        dst = self.third.at[h, st, self.landing(g)]
        return send(self.done.at[g, h, st], dst, self.sent.at[1], self.z_recv.at[h, st], self.place.at(z=ORDER[g]))

    def arrivals(self, g, st, h):
        ref = (self.pair_third if (g, st, h) in MIDDLE else self.third).at[h, st]
        return send(ref, ref, self.sent.at[1], self.z_recv.at[h, st], self.place.at(z=(self.place.z + 1) % 4))

    def half_pair(self, h):
        here = self.place
        return (slice(None), 1 - here.x) if h == 0 else (1 - here.y, slice(None))

    def inner(self, h):
        return self.place.y if h == 0 else self.place.x

    def pair_hop(self, g, st, h):
        src = self.parts.at[(g, h, st, *self.half_pair(h))]
        return send(src, self.first.at[g, h, st], self.sent.at[0], self.first_recv.at[g, h, st], self.place.first_link(h))

    def pair_across(self, g, st, h):
        dst = self.pair_third.at[h, st, self.landing(g)]
        return send(self.pair.at[g, h, st], dst, self.sent.at[1], self.z_recv.at[h, st], self.place.at(z=ORDER[g]))

    def last_hop(self, g, st, h):
        src, dst = self.pair.at[g, h, st, 1 - self.inner(h)], self.last_two.at[g, h, st, 1]
        return send(src, dst, self.sent.at[0], self.last_recv.at[g, h, st], self.place.second_link(h))

    def start(self, g, st, h, product):
        self.parts[g, h, st] = product.reshape(self.parts.shape[3:])
        if (g, st, h) in MIDDLE:
            self.pair_hop(g, st, h).start()
        else:
            self.hop(g, st, h, 0).start()

    def forward(self, g, st, h):
        here = self.place
        if (g, st, h) in MIDDLE:
            self.pair_hop(g, st, h).wait_recv()
            for i in range(2):
                y, x = (i, here.x) if h == 0 else (here.y, i)
                self.pair[g, h, st, i] = self.parts[g, h, st, y, x] + self.first[g, h, st, i]

            @pl.when(here.z != ORDER[g])
            def _():
                self.pair_across(g, st, h).start()

            return
        y, x = here.passed(h)
        self.hop(g, st, h, 0).wait_recv()
        self.total[g, h, st] = self.parts[g, h, st, y, x] + self.first[g, h, st, 0]
        self.hop(g, st, h, 2).start()
        self.hop(g, st, h, 1).start()

    def finish_xy(self, g, st, h):
        here = self.place
        if (g, st, h) in MIDDLE:

            @pl.when(here.z == ORDER[g])
            def _():
                self.arrivals(g, st, h).wait_recv()
                value = self.pair[g, h, st]
                for j in (0, 2, 1):
                    value = value + self.pair_third[h, st, j]
                self.pair[g, h, st] = value
                self.last_hop(g, st, h).start()

            return
        y, x = here.quarter(3)
        self.both_last(g, st, h).wait_recv()
        self.done[g, h, st] = (self.parts[g, h, st, y, x] + self.last_two[g, h, st, 0]) + self.last_two[g, h, st, 1]

        @pl.when(here.z != ORDER[g])
        def _():
            self.across(g, st, h).start()

    def result(self, g, st, h, out):
        here = self.place

        @pl.when(here.z == ORDER[g])
        def _():
            if (g, st, h) in MIDDLE:
                self.last_hop(g, st, h).wait_recv()
                out[:, self.columns(st, h)] = self.pair[g, h, st, self.inner(h)] + self.last_two[g, h, st, 1]
                return
            self.arrivals(g, st, h).wait_recv()
            value = self.done[g, h, st]
            for j in (0, 2, 1):
                value = value + self.third[h, st, j]
            out[:, self.columns(st, h)] = value

    def drain(self):
        here = self.place
        units = [(g, st, h) for g in range(len(ORDER)) for st in range(STRIPES) for h in range(2)]

        def sent_bytes(n, count):
            ref = self.measure.at[pl.ds(0, self.parts.shape[-2] * count), pl.ds(0, self.width)]
            send(ref, ref, self.sent.at[n], self.first_recv.at[0, 0, 0], here.at(col=1 - here.col)).wait_send()

        for own, z in enumerate(ORDER):

            @pl.when(here.z == z)
            def _():
                sent_bytes(0, sum(3 if u not in MIDDLE else 3 if u[0] == own else 2 for u in units))
                sent_bytes(1, sum(2 if u in MIDDLE else 1 for u in units if u[0] != own))


def kernel(window, env_hbm, site_hbm, out, env, site, high_site, low_site, windows, pan, lhs, *rest):
    env_sem, site_sem, win_send, win_recv, ready = rest[:5]
    bond_refs, panel_refs = rest[5:19], rest[19:31]
    here = Place()
    barrier = pltpu.get_barrier_semaphore()
    chips = [here.at(x=1 - here.x, col=0), here.at(y=1 - here.y, col=0)]
    chips += [here.at(z=(here.z + j) % 4, col=0) for j in range(1, 4)]
    first = here.col == 0
    second = jnp.logical_not(first)

    def signal(semaphore, device):
        pl.semaphore_signal(semaphore, inc=1, device_id=device, device_id_type=pl.DeviceIdType.MESH)

    @pl.when(first)
    def _():
        signal(barrier, here.at(col=1))

    for chip in chips:
        signal(barrier, chip)

    depth_local = env.shape[0]
    bond, panel = Bond(here, bond_refs, env), Panel(here, panel_refs, env)
    height = bond.block.shape[2]

    def env_columns(i, slot):
        y, x = here.quarter(i)
        return pl.ds(pl.multiple_of((slot * 4 + y * 2 + x) * depth_local, 128), depth_local)

    def env_load(i, slot):
        at = (slice(None), env_columns(i, slot))
        return pltpu.make_async_copy(env_hbm.at[at], env.at[at], env_sem.at[i, slot])

    def site_load(phys):
        return pltpu.make_async_copy(site_hbm.at[phys], site.at[phys], site_sem.at[phys])

    for i in range(4):
        for slot in range(2):
            env_load(i, slot).start()
    for phys in range(PHYS):
        site_load(phys).start()

    exchange = send(window, windows, win_send, win_recv, here.at(col=1 - here.col))

    @pl.when(second)
    def _():
        pl.semaphore_wait(barrier, 1)
        signal(ready, here.at(col=0))

    @pl.when(first)
    def _():
        pl.semaphore_wait(ready, 1)

    exchange.start()
    exchange.wait_recv()
    for phys in range(PHYS):
        flipped = (window[phys] + windows[phys]).T
        for k, z in enumerate(ORDER):
            at = phys * PANEL + k * height
            high, low = split(flipped[z * height : (z + 1) * height])
            pan[at : at + height, :] = high
            pan[PHYS * PANEL + at : PHYS * PANEL + at + height, :] = low

    def quarter_block(i, slot):
        y, x = here.quarter(i)
        env_load(i, slot).wait()
        product = dot3(pan[...], *split(env[:, env_columns(i, slot)]))
        product = product.reshape(PHYS, len(ORDER), height, depth_local)
        for phys in range(PHYS):
            for k in range(len(ORDER)):
                bond.parts[phys, k, slot, y, x] = product[phys, k]

    step = 16

    def split_site(phys):
        site_load(phys).wait()

        def one(i, carry):
            at = pl.ds(pl.multiple_of(i * step, step), step)
            to = pl.ds(pl.multiple_of(phys * depth_local + i * step, step), step)
            high_site[to, :], low_site[to, :] = split(site[phys, at, :])
            return carry

        lax.fori_loop(0, depth_local // step, one, 0)

    def gather_block(g):
        bond.fetch(g)
        lhs[g] = jnp.concatenate(split(jnp.concatenate([bond.block[g, phys] for phys in range(PHYS)], axis=1)), axis=0)

    def panel_product(g, st, h):
        columns = panel.columns(st, h)
        panel.start(g, st, h, dot3(lhs[g], high_site[:, columns], low_site[:, columns]))

    def greet():
        @pl.when(first)
        def _():
            pl.semaphore_wait(barrier, 2 * len(chips))
            signal(ready, here.at(col=1))

        @pl.when(second)
        def _():
            pl.semaphore_wait(ready, 1)

    def drain():
        exchange.wait_send()
        bond.drain()
        panel.drain()

    run = {
        "B": greet,
        "E": drain,
        "Q": quarter_block,
        "W": split_site,
        "ZS": lambda k, h, i: bond.halve(h, k, i).start(),
        "ZB": lambda k, h: bond.add_pair(h, k, 1),
        "ZC": lambda k, h: bond.add_pair(h, k, 2),
        "SA": lambda k, h, slot: bond.start(h, k, slot),
        "F": lambda k, h, slot: bond.forward(h, k, slot),
        "C": lambda k, h, slot: bond.finish_xy(h, k, slot),
        "R": lambda k, h: bond.result(h, k),
        "D": gather_block,
        "PD": panel_product,
        "PF": panel.forward,
        "PC": panel.finish_xy,
        "PR": lambda g, st, h: panel.result(g, st, h, out),
    }
    for name, *at in STEPS:
        run[name](*at)


def panel_window(site_tensors, panel_offset):
    cols_local = site_tensors.shape[2]
    padded = jnp.pad(site_tensors, ((0, 0), (0, 0), (PANEL, PANEL)))
    slice_start = jnp.clip(panel_offset[0] - lax.axis_index("col") * cols_local + PANEL, 0, cols_local + PANEL)
    return lax.dynamic_slice_in_dim(padded, slice_start, PANEL, 2)


def one_kernel(environment, site_tensors, panel_offset):
    depth_local, cols_local = environment.shape
    depth = len(ORDER)
    height = PANEL // depth
    any_space = pl.BlockSpec(memory_space=pl.ANY)
    in_vmem = pl.BlockSpec(memory_space=pltpu.VMEM)
    return pl.pallas_call(
        kernel,
        out_shape=jax.ShapeDtypeStruct((height // 4, cols_local), F32),
        in_specs=[in_vmem, any_space, any_space],
        out_specs=in_vmem,
        scratch_shapes=[
            pltpu.VMEM(environment.shape, F32),
            pltpu.VMEM(site_tensors.shape, F32),
            pltpu.VMEM((PHYS * depth_local, cols_local), BF16),
            pltpu.VMEM((PHYS * depth_local, cols_local), BF16),
            pltpu.VMEM((PHYS, depth_local, PANEL), F32),
            pltpu.VMEM((2 * PHYS * PANEL, depth_local), BF16),
            pltpu.VMEM((depth, 2 * height, PHYS * depth_local), BF16),
            pltpu.SemaphoreType.DMA((4, 2)),
            pltpu.SemaphoreType.DMA((PHYS,)),
            pltpu.SemaphoreType.DMA,
            pltpu.SemaphoreType.DMA,
            pltpu.SemaphoreType.REGULAR,
        ]
        + Bond.scratch(depth, height, depth_local)
        + Panel.scratch(depth, height // 4, cols_local // (2 * STRIPES)),
        compiler_params=pltpu.CompilerParams(collective_id=0, has_side_effects=True, vmem_limit_bytes=50 * 1024 * 1024),
    )(panel_window(site_tensors, panel_offset), environment, site_tensors)


def collectives(environment, site_tensors, panel_offset):
    rows_local, cols_local = environment.shape
    col_index = lax.axis_index("col")
    panel_rows = lax.psum(panel_window(site_tensors, panel_offset), "col")
    first_col = lax.axis_index("row") * rows_local
    owner_col = first_col // cols_local
    owner_mask = (col_index == owner_col).astype(F32)
    accumulated = jnp.zeros((PANEL, cols_local), F32)
    for phys in range(PHYS):
        partial_one = jnp.dot(
            panel_rows[phys].T, environment, precision=lax.Precision.HIGHEST, preferred_element_type=F32
        )
        block_one = lax.dynamic_slice_in_dim(lax.psum(partial_one, "row"), first_col - owner_col * cols_local, rows_local, 1)
        fetched_one = lax.psum(block_one * owner_mask, "col")
        accumulated = accumulated + jnp.dot(
            fetched_one, site_tensors[phys], precision=lax.Precision.HIGHEST, preferred_element_type=F32
        )
    return lax.psum_scatter(accumulated, "row", scatter_dimension=0, tiled=True)


def solution(mesh):
    rows, cols = mesh.shape["row"], mesh.shape["col"]

    def shards(environment, site_tensors, panel_offset):
        depth_local, cols_local = environment.shape
        fits = (
            rows == 4 * len(ORDER)
            and cols == 2
            and depth_local % 128 == 0
            and cols_local == 8 * depth_local
            and cols_local % (2 * STRIPES * 128) == 0
            and depth_local >= 8 * 6 * PHYS * len(ORDER)
            and depth_local >= 8 * 12 * STRIPES * 2
            and PANEL % (8 * rows) == 0
        )
        if fits:
            return one_kernel(environment, site_tensors, panel_offset)
        return collectives(environment, site_tensors, panel_offset)

    return jax.shard_map(
        shards,
        mesh=mesh,
        in_specs=(P("row", "col"), P(None, "row", "col"), P()),
        out_specs=P("row", "col"),
        check_vma=False,
    )
```
